32 devices in a mesh: bins: 8 (over z, x), lat: 4 (over y, core).
Axes of the slice: x: 2, y: 2, z: 4, core: 2. Of those that a mesh axis runs over, the one named last changes fastest.
Arguments:
- spectrum: float32 [1152, 64, 384], P('bins', 'lat'), may hold values from 0.05 to 2
- sea_mask: int32 [64, 384], P('lat'), may hold values 0 or 1
- current: float32 [768, 128], P('bins', 'lat'), may hold values from -0.6 to 0.6
- partner_plus: int32 [1152], replicated, may hold values from 0 to 1151
- partner_minus: int32 [1152], replicated, may hold values from 0 to 1151
- source_map: int32 [768, 128], P('bins', 'lat'), may hold values from 0 to 8
Outputs:
- spectrum_out: float32 [1152, 64, 384], P('bins', 'lat')
- stokes: float32 [2, 64, 768, 128], P(None, None, 'bins', 'lat')
The draws below stay inside these ranges and needn't reach their ends.
All inputs are finite; a program needn't handle non-finite values. No bound on the sum of `sea_mask` on one device may be relied on, other than what follows from the above.
Results may differ from the reference program's by a relative error of at most 0.000086.
Values sent between devices are 32-bit elements; how exact they have to be, the bound alone decides.
A program may use at most 128 MiB of HBM per device.

```python
import math
import jax
import jax.numpy as jnp
from jax import lax

NDIR = 36
NFREQ = 32
LEV = 64
NLON = 384
BINS = 1152
NLAT = 64


def with_ends(values, key, low, top_value):
    extent = values.shape
    index_at = [jax.random.randint(jax.random.fold_in(key, axis), (), 0, extent[axis]) for axis in range(len(extent))]
    values = values.at[tuple(index_at)].set(low)
    longest = extent.index(max(extent))
    index_at[longest] = (index_at[longest] + 1) % extent[longest]
    return values.at[tuple(index_at)].set(top_value)


def block_levels(key, shape, split, low, high):
    gain = 1.0
    for axis_at, shards_of in split:
        heights = jax.random.uniform(jax.random.fold_in(jax.random.fold_in(key, 6), axis_at), (shards_of,), jnp.float32, low / len(split), high / len(split))
        gain = gain * jnp.repeat(jnp.exp(heights), shape[axis_at] // shards_of).reshape((-1,) + (1,) * (len(shape) - 1 - axis_at))
    return gain


def gaussian(key, dims, deviation, limit, cuts=(), held_as=jnp.bfloat16):
    values = deviation * jax.random.normal(key, dims, jnp.float32)
    if cuts:
        values = values * block_levels(key, dims, cuts, -0.22, 0.18)
    return jnp.clip(values, -limit, limit).astype(held_as)


def setup_inputs(seed: int = 0) -> dict:
    keys = jax.random.split(jax.random.key(seed), 7)
    return {
        "spectrum": jnp.clip(jnp.exp(math.log(2.0) - 3.6888794 * jax.random.uniform(keys[0], (BINS, NLAT, NLON), jnp.float32) ** block_levels(keys[0], (BINS, NLAT, NLON), ((0, 8), (1, 4)), -0.2, 0.2)), 0.05, 2.0),
        "sea_mask": with_ends((jax.random.randint(keys[1], (NLAT, NLON), 0, 5) < 4).astype(jnp.int32), jax.random.fold_in(keys[1], 1), 0, 1),
        "current": gaussian(keys[2], (2 * NLON, 2 * NLAT), 0.15, 0.6, ((0, 8), (1, 4)), jnp.float32),
        "partner_plus": with_ends(jax.random.randint(keys[3], (BINS,), 0, BINS), jax.random.fold_in(keys[3], 1), 0, BINS - 1).astype(jnp.int32),
        "partner_minus": with_ends(jax.random.randint(keys[4], (BINS,), 0, BINS), jax.random.fold_in(keys[4], 1), 0, BINS - 1).astype(jnp.int32),
        "source_map": with_ends(jax.random.randint(keys[5], (2 * NLON, 2 * NLAT), 0, 9), jax.random.fold_in(keys[5], 1), 0, 8).astype(jnp.int32),
    }


HIGHEST = lax.Precision.HIGHEST

def bin_tables():
    dir_index = jnp.arange(NDIR, dtype=jnp.float32)
    freq_index = jnp.arange(NFREQ, dtype=jnp.float32)
    angles = 2.0 * math.pi * (dir_index + 0.5) / NDIR
    speeds = 0.12 + 0.25 * (NFREQ - 1 - freq_index) / (NFREQ - 1)
    along_x = jnp.repeat(speeds, NDIR) * jnp.tile(jnp.cos(angles), NFREQ)
    along_y = jnp.repeat(speeds, NDIR) * jnp.tile(jnp.sin(angles), NFREQ)
    strength = jnp.repeat(0.06 * (1.0 + freq_index / (NFREQ - 1)), NDIR)
    levels = jnp.arange(LEV, dtype=jnp.float32) + 0.5
    wavenumber = 0.02 * jnp.power(1.15, freq_index)
    decay = jnp.repeat(jnp.exp(-levels[:, None] * wavenumber[None, :]), NDIR, axis=1)
    amplitude = 2.0 / math.sqrt(NDIR * NFREQ)
    cosines = jnp.tile(jnp.cos(angles), NFREQ)
    sines = jnp.tile(jnp.sin(angles), NFREQ)
    drift_table = amplitude * jnp.concatenate([decay * cosines[None, :], decay * sines[None, :]], axis=0)
    return (along_x, along_y, strength, drift_table)

def cell_means(current_cells):
    lon_count = current_cells.shape[0] // 2
    lat_count = current_cells.shape[1] // 2
    return current_cells.reshape(lon_count, 2, lat_count, 2).mean(axis=(1, 3))

def face_fluxes(padded, velocity, dimension):
    face_count = padded.shape[dimension] - 3

    def section(low_edge):
        return lax.slice_in_dim(padded, low_edge, low_edge + face_count, axis=dimension)
    left_value = (-section(0) + 5.0 * section(1) + 2.0 * section(2)) / 6.0
    right_value = (2.0 * section(1) + 5.0 * section(2) - section(3)) / 6.0
    return jnp.maximum(velocity, 0.0) * left_value + jnp.minimum(velocity, 0.0) * right_value

def transport(padded_rows, zonal_flow, along_x, along_y, sea_cells):
    row_count = padded_rows.shape[1] - 4
    spectra = padded_rows[:, 2:2 + row_count, :]
    padded_cols = jnp.pad(spectra, ((0, 0), (0, 0), (2, 2)))
    zonal_padded = jnp.pad(zonal_flow, ((0, 0), (1, 1)))
    face_zonal = 0.5 * (zonal_padded[:, :-1] + zonal_padded[:, 1:])
    speed_x = along_x[:, None, None] + face_zonal[None, :, :]
    flux_x = face_fluxes(padded_cols, speed_x, 2)
    flux_y = face_fluxes(padded_rows, along_y[:, None, None], 1)
    change = flux_x[:, :, 1:] - flux_x[:, :, :-1] + flux_y[:, 1:, :] - flux_y[:, :-1, :]
    return sea_cells[None, :, :] * (spectra - change)

def transport_all(spectra, zonal_flow, along_x, along_y, sea_cells):
    grouped = spectra.reshape(NFREQ, NDIR, NLAT, NLON)

    def one_bundle(entries):
        bundle, speed_x, speed_y = entries
        padded = jnp.pad(bundle, ((0, 0), (2, 2), (0, 0)))
        return transport(padded, zonal_flow, speed_x, speed_y, sea_cells)
    carried = lax.map(one_bundle, (grouped, along_x.reshape(NFREQ, NDIR), along_y.reshape(NFREQ, NDIR)))
    return carried.reshape(NDIR * NFREQ, NLAT, NLON)

def spread_to_ocean(rim, source_map):
    row_count = rim.shape[1] - 2
    col_count = rim.shape[2] - 2
    result = jnp.zeros((rim.shape[0], 2 * col_count, 2 * row_count), jnp.float32)
    for offset in range(9):
        row_shift = offset // 3 - 1
        col_shift = offset % 3 - 1
        shifted = rim[:, 1 + row_shift:1 + row_shift + row_count, 1 + col_shift:1 + col_shift + col_count]
        shifted = jnp.swapaxes(shifted, 1, 2)
        shifted = jnp.repeat(jnp.repeat(shifted, 2, axis=1), 2, axis=2)
        result = result + jnp.where(source_map[None, :, :] == offset, shifted, jnp.float32(0.0))
    return result

def reference(spectrum, sea_mask, current, partner_plus, partner_minus, source_map):
    along_x, along_y, strength, drift_table = bin_tables()
    sea_cells = sea_mask.astype(jnp.float32)
    zonal_flow = cell_means(current).T
    masked = spectrum * sea_cells[None, :, :]
    after_first = transport_all(masked, zonal_flow, along_x, along_y, sea_cells)
    bin_count = NDIR * NFREQ
    flat_rows = after_first.reshape(bin_count, NLAT * NLON)
    plus_part = jnp.take(flat_rows, partner_plus, axis=0)
    minus_part = jnp.take(flat_rows, partner_minus, axis=0)
    source = strength[:, None] * (flat_rows * flat_rows * (plus_part + minus_part) - 2.0 * flat_rows * plus_part * minus_part)
    back = jax.ops.segment_sum(source, partner_plus, num_segments=bin_count) + jax.ops.segment_sum(source, partner_minus, num_segments=bin_count)
    middle = flat_rows + (source - 0.5 * back)
    drift_rows = jnp.dot(drift_table, middle, precision=HIGHEST).reshape(2 * LEV, NLAT, NLON)
    rim = jnp.pad(drift_rows, ((0, 0), (1, 1), (1, 1)))
    stokes = spread_to_ocean(rim, source_map).reshape(2, LEV, 2 * NLON, 2 * NLAT)
    second = transport_all(middle.reshape(bin_count, NLAT, NLON), zonal_flow, along_x, along_y, sea_cells)
    return (second, stokes)
```

```python
import functools
import math

import jax
import jax.numpy as jnp
import numpy as np
from jax import lax
from jax.experimental import pallas as pl
from jax.experimental.pallas import tpu as pltpu
from jax.sharding import PartitionSpec as P

NDIR = 36
NFREQ = 32
LEV = 64


HIGHEST = lax.Precision.HIGHEST


def extended(block, sides, width):
    for axis, dim in sides:
        count = lax.axis_size(axis)
        forward = [(i, i + 1) for i in range(count - 1)]
        backward = [(target, source) for source, target in forward]
        low = lax.ppermute(
            lax.slice_in_dim(block, block.shape[dim] - width, None, axis=dim), axis, forward
        )
        high = lax.ppermute(lax.slice_in_dim(block, 0, width, axis=dim), axis, backward)
        block = jnp.concatenate([low, block, high], axis=dim)
    return block


def bin_tables():
    dir_index = jnp.arange(NDIR, dtype=jnp.float32)
    freq_index = jnp.arange(NFREQ, dtype=jnp.float32)
    angles = 2.0 * math.pi * (dir_index + 0.5) / NDIR
    speeds = 0.12 + 0.25 * (NFREQ - 1 - freq_index) / (NFREQ - 1)
    along_x = jnp.repeat(speeds, NDIR) * jnp.tile(jnp.cos(angles), NFREQ)
    along_y = jnp.repeat(speeds, NDIR) * jnp.tile(jnp.sin(angles), NFREQ)
    strength = jnp.repeat(0.06 * (1.0 + freq_index / (NFREQ - 1)), NDIR)
    levels = jnp.arange(LEV, dtype=jnp.float32) + 0.5
    wavenumber = 0.02 * jnp.power(1.15, freq_index)
    decay = jnp.repeat(jnp.exp(-levels[:, None] * wavenumber[None, :]), NDIR, axis=1)
    amplitude = 2.0 / math.sqrt(NDIR * NFREQ)
    cosines = jnp.tile(jnp.cos(angles), NFREQ)
    sines = jnp.tile(jnp.sin(angles), NFREQ)
    drift_table = amplitude * jnp.concatenate(
        [decay * cosines[None, :], decay * sines[None, :]], axis=0
    )
    return (along_x, along_y, strength, drift_table)


def fixed_tables():
    dir_index = np.arange(NDIR, dtype=np.float32)
    freq_index = np.arange(NFREQ, dtype=np.float32)
    angles = 2.0 * math.pi * (dir_index + 0.5) / NDIR
    speeds = 0.12 + 0.25 * (NFREQ - 1 - freq_index) / (NFREQ - 1)
    along_x = np.repeat(speeds, NDIR) * np.tile(np.cos(angles), NFREQ)
    along_y = np.repeat(speeds, NDIR) * np.tile(np.sin(angles), NFREQ)
    strength = np.repeat(0.06 * (1.0 + freq_index / (NFREQ - 1)), NDIR)
    levels = np.arange(LEV, dtype=np.float32) + 0.5
    wavenumber = 0.02 * np.power(np.float32(1.15), freq_index)
    decay = np.repeat(np.exp(-levels[:, None] * wavenumber[None, :]), NDIR, axis=1)
    amplitude = 2.0 / math.sqrt(NDIR * NFREQ)
    cosines = np.tile(np.cos(angles), NFREQ)
    sines = np.tile(np.sin(angles), NFREQ)
    drift_table = amplitude * np.concatenate(
        [decay * cosines[None, :], decay * sines[None, :]], axis=0
    )
    tables = (along_x, along_y, strength, drift_table)
    return tuple(np.asarray(table, dtype=np.float32) for table in tables)


def cell_means(current_cells):
    lon_count = current_cells.shape[0] // 2
    lat_count = current_cells.shape[1] // 2
    return current_cells.reshape(lon_count, 2, lat_count, 2).mean(axis=(1, 3))


def face_fluxes(padded, velocity, dimension):
    face_count = padded.shape[dimension] - 3

    def section(low_edge):
        return lax.slice_in_dim(padded, low_edge, low_edge + face_count, axis=dimension)

    left_value = (-section(0) + 5.0 * section(1) + 2.0 * section(2)) / 6.0
    right_value = (2.0 * section(1) + 5.0 * section(2) - section(3)) / 6.0
    return jnp.maximum(velocity, 0.0) * left_value + jnp.minimum(velocity, 0.0) * right_value


def transport(padded_rows, zonal_flow, along_x, along_y, sea_cells):
    row_count = padded_rows.shape[1] - 4
    spectra = padded_rows[:, 2 : 2 + row_count, :]
    padded_cols = jnp.pad(spectra, ((0, 0), (0, 0), (2, 2)))
    zonal_padded = jnp.pad(zonal_flow, ((0, 0), (1, 1)))
    face_zonal = 0.5 * (zonal_padded[:, :-1] + zonal_padded[:, 1:])
    speed_x = along_x[:, None, None] + face_zonal[None, :, :]
    flux_x = face_fluxes(padded_cols, speed_x, 2)
    flux_y = face_fluxes(padded_rows, along_y[:, None, None], 1)
    change = flux_x[:, :, 1:] - flux_x[:, :, :-1] + flux_y[:, 1:, :] - flux_y[:, :-1, :]
    return sea_cells[None, :, :] * (spectra - change)


def spread_to_ocean(rim, source_map):
    row_count = rim.shape[1] - 2
    col_count = rim.shape[2] - 2
    result = jnp.zeros((rim.shape[0], 2 * col_count, 2 * row_count), jnp.float32)
    for offset in range(9):
        row_shift = offset // 3 - 1
        col_shift = offset % 3 - 1
        shifted = rim[
            :, 1 + row_shift : 1 + row_shift + row_count, 1 + col_shift : 1 + col_shift + col_count
        ]
        shifted = jnp.swapaxes(shifted, 1, 2)
        shifted = jnp.repeat(jnp.repeat(shifted, 2, axis=1), 2, axis=2)
        result = result + jnp.where(source_map[None, :, :] == offset, shifted, jnp.float32(0.0))
    return result


def on_device_plain(spectrum, sea_mask, current, partner_plus, partner_minus, source_map):
    along_x, along_y, strength, drift_table = bin_tables()
    bin_count = NDIR * NFREQ
    local_bins = spectrum.shape[0]
    first_bin = lax.axis_index("bins") * local_bins
    local_x = lax.dynamic_slice_in_dim(along_x, first_bin, local_bins)
    local_y = lax.dynamic_slice_in_dim(along_y, first_bin, local_bins)
    sea_cells = sea_mask.astype(jnp.float32)
    strip_flow = cell_means(current)
    zonal_flow = lax.all_gather(strip_flow, "bins", axis=0, tiled=True).T
    masked = spectrum * sea_cells[None, :, :]
    padded = extended(masked, (("lat", 1),), 2)
    after_first = transport(padded, zonal_flow, local_x, local_y, sea_cells)
    bin_ids = jnp.arange(bin_count, dtype=jnp.int32)
    plus_table = (partner_plus[:, None] == bin_ids[None, :]).astype(jnp.float32)
    minus_table = (partner_minus[:, None] == bin_ids[None, :]).astype(jnp.float32)
    contract_first = (((0,), (0,)), ((), ()))
    arrived = lax.all_to_all(after_first, "bins", split_axis=2, concat_axis=0, tiled=True)
    row_count = arrived.shape[1]
    col_count = arrived.shape[2]
    flat_rows = arrived.reshape(bin_count, row_count * col_count)
    plus_part = jnp.dot(plus_table, flat_rows, precision=HIGHEST)
    minus_part = jnp.dot(minus_table, flat_rows, precision=HIGHEST)
    source = strength[:, None] * (
        flat_rows * flat_rows * (plus_part + minus_part) - 2.0 * flat_rows * plus_part * minus_part
    )
    back = lax.dot_general(plus_table, source, contract_first, precision=HIGHEST) + lax.dot_general(
        minus_table, source, contract_first, precision=HIGHEST
    )
    middle = flat_rows + (source - 0.5 * back)
    drift_rows = jnp.dot(drift_table, middle, precision=HIGHEST)
    middle, drift_rows = (
        middle.reshape(bin_count, row_count, col_count),
        drift_rows.reshape(2 * LEV, row_count, col_count),
    )
    rim = extended(drift_rows, (("bins", 2), ("lat", 1)), 1)
    ocean = spread_to_ocean(rim, source_map)
    stokes = ocean.reshape(2, LEV, ocean.shape[1], ocean.shape[2])
    returned = lax.all_to_all(middle, "bins", split_axis=0, concat_axis=2, tiled=True)
    padded_again = extended(returned, (("lat", 1),), 2)
    second = transport(padded_again, zonal_flow, local_x, local_y, sea_cells)
    return (second, stokes)

MESH = pl.DeviceIdType.MESH
TILE = 128
GROUP = 8
LANES = TILE // GROUP
VMEM = pltpu.VMEM
FORTH = 3
HOME = 6
F32 = jnp.float32


def row_groups(rows):
    edge = rows // 4
    inner = list(range(edge, rows - edge))
    return inner, list(range(edge)) + list(range(rows - edge, rows))


def turn_blocks(tiles):
    lane = lax.broadcasted_iota(jnp.int32, tiles[0].shape, 1) // LANES
    tiles = list(tiles)
    step = 1
    while step < GROUP:
        clear = lax.rem(lane // step, 2) == 0
        for i in range(GROUP):
            if i & step:
                continue
            upper, lower = tiles[i], tiles[i + step]
            tiles[i] = jnp.where(clear, upper, pltpu.roll(lower, step * LANES, 1))
            tiles[i + step] = jnp.where(clear, pltpu.roll(upper, TILE - step * LANES, 1), lower)
        step *= 2
    return tiles


def advect(get, wanted, coefs, face, half, mask):
    cols = face.shape[1]
    lane = lax.broadcasted_iota(jnp.int32, (8, cols), 1)
    at_first = lane == 0
    at_second = lane <= 1
    at_last = lane == cols - 1
    sixth = F32(1.0 / 6.0)
    coef = [jnp.broadcast_to(coefs[:, i : i + 1], (8, cols)) for i in range(6)]
    cache = {}

    def f(row):
        if row not in cache:
            cache[row] = get(row)
        return cache[row]

    results = []
    for row in wanted:
        c = f(row)
        m1 = jnp.where(at_first, 0.0, pltpu.roll(c, 1, 1))
        m2 = jnp.where(at_second, 0.0, pltpu.roll(c, 2, 1))
        p1 = jnp.where(at_last, 0.0, pltpu.roll(c, cols - 1, 1))
        speed = coef[0] + face[row : row + 1, :]
        ahead = speed > 0.0
        part = 3.0 * jnp.where(ahead, m1, c) - jnp.where(ahead, m2, p1)
        flux = (speed * sixth) * (part + 2.0 * (m1 + c))
        end_speed = coef[0] + half[row : row + 1, :]
        end = (end_speed * sixth) * jnp.where(end_speed > 0.0, 5.0 * c - m1, 2.0 * c)
        upper = jnp.where(at_last, end, pltpu.roll(flux, cols - 1, 1))
        along_y = (
            coef[1] * f(row - 2)
            + coef[2] * f(row - 1)
            + coef[3] * c
            + coef[4] * f(row + 1)
            + coef[5] * f(row + 2)
        )
        results.append(mask[row : row + 1, :] * (c - ((upper - flux) + along_y)))
    return results


def halves(value):
    high = value.astype(jnp.bfloat16)
    return high, (value - high.astype(F32)).astype(jnp.bfloat16)


def step_kernel(
    count,
    bands,
    x_ref,
    mask_ref,
    current_ref,
    partner_ref,
    source_ref,
    coef_ref,
    drift_ref,
    out_ref,
    stokes_ref,
    block,
    by_row,
    leaving,
    arrived,
    middle,
    returned,
    plus_table,
    minus_table,
    back_table,
    parts,
    source_parts,
    total,
    mask,
    half,
    face,
    strips,
    low_halo,
    high_halo,
    low_again,
    high_again,
    near,
    chosen_map,
    ocean,
    load_sem,
    strip_send,
    strip_recv,
    halo_send,
    halo_recv,
    in_send,
    in_recv,
    back_send,
    back_recv,
    again_send,
    again_recv,
    near_send,
    near_recv,
    out_sem,
    ocean_sem,
):
    me = lax.axis_index("bins")
    band = lax.axis_index("lat")
    local, rows, cols = block.shape
    bins = local * count
    strip = cols // count
    each = strip // LANES
    pieces = cols // LANES
    chunk_in = local // FORTH
    chunk_out = local // HOME
    tiles = bins // TILE
    width = each * TILE
    across = cols // TILE
    groups = row_groups(rows)
    below = lax.rem(band + bands - 1, bands)
    above = lax.rem(band + 1, bands)
    left = lax.rem(me + count - 1, count)
    right = lax.rem(me + 1, count)
    edges = (jnp.where(band > 0, F32(1.0), F32(0.0)), jnp.where(band < bands - 1, F32(1.0), F32(0.0)))

    def remote(src, dst, send_sem, recv_sem, peer, axis="bins"):
        return pltpu.make_async_remote_copy(
            src_ref=src,
            dst_ref=dst,
            send_sem=send_sem,
            recv_sem=recv_sem,
            device_id={axis: peer},
            device_id_type=MESH,
        )

    def load_copy(part):
        here = pl.ds(part * chunk_in, chunk_in)
        return pltpu.make_async_copy(x_ref.at[here], block.at[here], load_sem.at[part])

    for part in range(FORTH):
        load_copy(part).start()

    barrier = pltpu.get_barrier_semaphore()
    for step in range(1, count):
        pl.semaphore_signal(
            barrier,
            inc=1,
            device_id={"bins": lax.rem(me + step, count)},
            device_id_type=MESH,
        )
    for peer in (below, above):
        pl.semaphore_signal(barrier, inc=1, device_id={"lat": peer}, device_id_type=MESH)

    lons = current_ref.shape[1]
    pairs = current_ref[pl.ds(0, rows, stride=2), :] + current_ref[pl.ds(1, rows, stride=2), :]
    fold = lax.broadcasted_iota(jnp.int32, (lons, TILE), 0) // 2
    fold = jnp.where(fold == lax.broadcasted_iota(jnp.int32, (lons, TILE), 1), F32(0.125), F32(0.0))
    strips[me] = jnp.dot(pairs, fold, precision=HIGHEST, preferred_element_type=F32)
    mask[...] = mask_ref[...].astype(F32)

    pl.semaphore_wait(barrier, count + 1)

    def strip_copy(step):
        peer = lax.rem(me + step, count)
        return remote(strips.at[me], strips.at[me], strip_send.at[step], strip_recv.at[step], peer)

    for step in range(1, count):
        strip_copy(step).start()

    for part in range(FORTH):
        load_copy(part).wait()

        def turn_step(i, carry, part=part):
            here = pl.ds(pl.multiple_of(part * chunk_in + i * 8, 8), 8)
            turned = pltpu.einshape("brl->rbl", block[here, :, :] * mask[...][None])
            for row in range(rows):
                by_row[row, here, :] = turned[row]
            return carry

        lax.fori_loop(0, chunk_in // 8, turn_step, 0)

    halo_copies = [
        remote(
            by_row.at[pl.ds(0, 2)], high_halo, halo_send.at[0], halo_recv.at[0], below, "lat"
        ),
        remote(
            by_row.at[pl.ds(rows - 2, 2)], low_halo, halo_send.at[1], halo_recv.at[1], above, "lat"
        ),
    ]
    for copy in halo_copies:
        copy.start()
    for step in range(1, count):
        strip_copy(step).wait()
    spread = jnp.zeros((rows, cols), F32)
    rest = jnp.zeros((rows, cols - TILE), F32)
    for peer in range(count):
        piece = jnp.concatenate([strips[peer], rest], axis=1)
        spread = spread + (pltpu.roll(piece, peer * strip, 1) if peer else piece)
    half[...] = spread
    first_lane = lax.broadcasted_iota(jnp.int32, (rows, cols), 1) == 0
    face[...] = spread + jnp.where(first_lane, 0.0, pltpu.roll(spread, 1, 1))
    first_bin = me * local

    def fetch(here, low, high):
        def get(row):
            if row < 0:
                return edges[0] * low[row + 2, here, :]
            if row >= rows:
                return edges[1] * high[row - rows, here, :]
            return by_row[row, here, :]

        return get

    def coefs_at(start):
        return coef_ref[pl.ds(pl.multiple_of(first_bin + start, 8), 8), :]

    def in_copy(h, part, step):
        peer = lax.rem(me + step, count)
        src = leaving.at[h, pl.ds(peer * each, each), pl.ds(pl.multiple_of(part * chunk_in, 8), chunk_in), :]
        dst = arrived.at[h, :, pl.ds(pl.multiple_of(first_bin + part * chunk_in, 8), chunk_in), :]
        if step == 0:
            return pltpu.make_async_copy(src, dst, in_recv.at[h, part, 0])
        return remote(src, dst, in_send.at[h, part, step], in_recv.at[h, part, step], peer)

    for h in range(2):
        if h == 1:
            for copy in halo_copies:
                copy.wait()

        def forth_part(part, carry, h=h):
            def forth_step(i, carry):
                start = part * chunk_in + i * 8
                here = pl.ds(pl.multiple_of(start, 8), 8)
                found = advect(
                    fetch(here, low_halo, high_halo),
                    groups[h],
                    coefs_at(start),
                    face[...],
                    half[...],
                    mask[...],
                )
                for t in range(across):
                    turned = turn_blocks([row[:, t * TILE : (t + 1) * TILE] for row in found])
                    for q in range(GROUP):
                        leaving[h, t * GROUP + q, here, :] = turned[q]
                return carry

            lax.fori_loop(0, chunk_in // 8, forth_step, 0)
            for step in range(count):
                in_copy(h, part, step).start()
            return carry

        lax.fori_loop(0, FORTH, forth_part, 0)

    def table_step(tile, carry):
        here = pl.ds(pl.multiple_of(tile * TILE, TILE), TILE)
        along = lax.broadcasted_iota(jnp.int32, (TILE, bins), 1).astype(F32)
        down = (lax.broadcasted_iota(jnp.int32, (TILE, bins), 0) + tile * TILE).astype(F32)
        one = F32(1.0)
        zero = F32(0.0)
        back = jnp.zeros((TILE, bins), F32)
        for which, table in ((0, plus_table), (1, minus_table)):
            column = jnp.broadcast_to(partner_ref[which : which + 1, here], (TILE, TILE)).astype(F32).T
            column = jnp.concatenate([column] * tiles, axis=1)
            table[here, :] = jnp.where(column == along, one, zero).astype(jnp.bfloat16)
            whole = partner_ref[which : which + 1, :].astype(F32)
            back = back + jnp.where(whole == down, one, zero)
        back_table[here, :] = back.astype(jnp.bfloat16)
        return carry

    lax.fori_loop(0, tiles, table_step, 0)

    def back_copy(h, part, step):
        peer = lax.rem(me + step, count)
        src = middle.at[h, :, pl.ds(pl.multiple_of(peer * local + part * chunk_out, 8), chunk_out), :]
        dst = returned.at[h, pl.ds(me * each, each), pl.ds(pl.multiple_of(part * chunk_out, 8), chunk_out), :]
        if step == 0:
            return pltpu.make_async_copy(src, dst, back_recv.at[h, part, 0])
        return remote(src, dst, back_send.at[h, part, step], back_recv.at[h, part, step], peer)

    def pick(table, here, value):
        both = jnp.dot(table[here, :], value[...], preferred_element_type=F32)
        return both[:, :width] + both[:, width:]

    def near_copy(slot):
        if slot == 0:
            src, dst, peer, axis = near.at[pl.ds(1, rows), pl.ds(8, 8)], near.at[pl.ds(1, rows), pl.ds(8 + strip, 8)], left, "bins"
        elif slot == 1:
            src, dst, peer, axis = near.at[pl.ds(1, rows), pl.ds(strip, 8)], near.at[pl.ds(1, rows), pl.ds(0, 8)], right, "bins"
        elif slot == 2:
            src, dst, peer, axis = near.at[1], near.at[rows + 1], below, "lat"
        else:
            src, dst, peer, axis = near.at[rows], near.at[0], above, "lat"
        return remote(src, dst, near_send.at[slot], near_recv.at[slot], peer, axis)

    for h in range(2):

        def await_in(part, carry, h=h):
            for step in range(count):
                in_copy(h, part, step).wait()
            return carry

        lax.fori_loop(0, FORTH, await_in, 0)

        def split_step(tile, carry, h=h):
            here = pl.ds(pl.multiple_of(tile * TILE, TILE), TILE)
            for g in range(each):
                upper, lower = halves(arrived[h, g, here, :])
                parts[here, g * TILE : (g + 1) * TILE] = upper
                parts[here, width + g * TILE : width + (g + 1) * TILE] = lower
            return carry

        lax.fori_loop(0, tiles, split_step, 0)

        def source_step(tile, carry, h=h):
            here = pl.ds(pl.multiple_of(tile * TILE, TILE), TILE)
            plus = pick(plus_table, here, parts)
            minus = pick(minus_table, here, parts)
            strength = coef_ref[here, 6:7]
            for g in range(each):
                lanes = slice(g * TILE, (g + 1) * TILE)
                own = arrived[h, g, here, :]
                p, m = plus[:, lanes], minus[:, lanes]
                source = strength * (own * own * (p + m) - 2.0 * own * p * m)
                upper, lower = halves(source)
                source_parts[here, lanes] = upper
                source_parts[here, width + g * TILE : width + (g + 1) * TILE] = lower
                middle[h, g, here, :] = own + source
            return carry

        lax.fori_loop(0, tiles, source_step, 0)
        total[...] = jnp.zeros_like(total)

        def back_step(tile, carry, h=h):
            here = pl.ds(pl.multiple_of(tile * TILE, TILE), TILE)
            back = pick(back_table, here, source_parts)
            done = []
            for g in range(each):
                value = middle[h, g, here, :] - 0.5 * back[:, g * TILE : (g + 1) * TILE]
                middle[h, g, here, :] = value
                done.append(value)
            total[...] += jnp.dot(
                drift_ref[:, here],
                jnp.concatenate(done, axis=1),
                precision=HIGHEST,
                preferred_element_type=F32,
            )
            return carry

        lax.fori_loop(0, tiles, back_step, 0)
        for g in range(each):
            points = total[:, g * TILE : (g + 1) * TILE].T
            for at, row in enumerate(groups[h]):
                near[1 + row, 8 + g * LANES : 8 + (g + 1) * LANES, :] = points[at * LANES : (at + 1) * LANES, :]
        if h == 1:
            near_copy(0).start()
            near_copy(1).start()

        def send_back(part, carry, h=h):
            for step in range(count):
                back_copy(h, part, step).start()
            return carry

        lax.fori_loop(0, HOME, send_back, 0)

    near_copy(0).wait()
    near_copy(1).wait()
    side = (jnp.where(me > 0, F32(1.0), F32(0.0)), jnp.where(me < count - 1, F32(1.0), F32(0.0)))
    inner = pl.ds(1, rows)
    near[inner, 0:8, :] = near[inner, 0:8, :] * side[0]
    near[inner, 8 + strip : 16 + strip, :] = near[inner, 8 + strip : 16 + strip, :] * side[1]
    near_copy(2).start()
    near_copy(3).start()

    chosen_map[...] = jnp.zeros_like(chosen_map)
    sources = source_ref[...]
    third = jnp.where(sources >= 3, 1, 0) + jnp.where(sources >= 6, 1, 0)
    extent = strip + 16
    columns = lax.broadcasted_iota(jnp.int32, sources.shape, 1) // 2
    chosen_map[:, :lons] = third * extent + 7 + columns + (sources - 3 * third)
    near_copy(2).wait()
    near_copy(3).wait()
    near[0] = near[0] * edges[0]
    near[rows + 1] = near[rows + 1] * edges[1]

    depth = 3 * extent
    profiles = near.shape[2]
    ocean_copies = []
    for octet in range(2 * rows // 8):
        found = []
        for row in range(octet * 4, octet * 4 + 4):
            window = near[row : row + 3].reshape(depth, profiles)
            down = lax.broadcasted_iota(jnp.int32, (depth, TILE), 0)
            chosen = [
                jnp.where(down == chosen_map[lat : lat + 1, :], F32(1.0), F32(0.0))
                for lat in (2 * row, 2 * row + 1)
            ]
            both = lax.dot_general(
                window,
                jnp.concatenate(chosen, axis=1),
                (((0,), (0,)), ((), ())),
                precision=HIGHEST,
                preferred_element_type=F32,
            )
            found += [both[:, :TILE], both[:, TILE:]]
        here = pl.ds(octet * 8, 8)
        ocean[:, here, :] = pltpu.einshape("ypl->pyl", jnp.stack(found))[:, :, :lons]
        copy = pltpu.make_async_copy(ocean.at[:, here, :], stokes_ref.at[:, here, :], ocean_sem.at[octet])
        copy.start()
        ocean_copies.append(copy)

    def again_copy(part, slot):
        here = pl.ds(pl.multiple_of(part * chunk_out, 8), chunk_out)
        if slot == 0:
            src, dst, peer = by_row.at[pl.ds(0, 2), here, :], high_again.at[:, here, :], below
        else:
            src, dst, peer = by_row.at[pl.ds(rows - 2, 2), here, :], low_again.at[:, here, :], above
        return remote(src, dst, again_send.at[slot, part], again_recv.at[slot, part], peer, "lat")

    def out_copy(part):
        here = pl.ds(part * chunk_out, chunk_out)
        return pltpu.make_async_copy(block.at[here], out_ref.at[here], out_sem.at[part])

    def home_part(turn, carry):
        @pl.when(turn < HOME)
        def _():
            for h in range(2):
                for step in range(count):
                    back_copy(h, turn, step).wait()

            def unpack_step(i, carry):
                here = pl.ds(pl.multiple_of(turn * chunk_out + i * 8, 8), 8)
                for h in range(2):
                    for t in range(across):
                        turned = turn_blocks([returned[h, t * GROUP + q, here, :] for q in range(GROUP)])
                        for at, row in enumerate(groups[h]):
                            by_row[row, here, t * TILE : (t + 1) * TILE] = turned[at]
                return carry

            lax.fori_loop(0, chunk_out // 8, unpack_step, 0)
            again_copy(turn, 0).start()
            again_copy(turn, 1).start()

        @pl.when(turn > 0)
        def _():
            part = turn - 1
            again_copy(part, 0).wait()
            again_copy(part, 1).wait()

            def home_step(i, carry):
                start = part * chunk_out + i * 8
                here = pl.ds(pl.multiple_of(start, 8), 8)
                found = advect(
                    fetch(here, low_again, high_again),
                    list(range(rows)),
                    coefs_at(start),
                    face[...],
                    half[...],
                    mask[...],
                )
                block[here, :, :] = pltpu.einshape("rbl->brl", jnp.stack(found))
                return carry

            lax.fori_loop(0, chunk_out // 8, home_step, 0)
            out_copy(part).start()

        return carry

    lax.fori_loop(0, HOME + 1, home_part, 0)
    for part in range(HOME):
        out_copy(part).wait()
    for copy in ocean_copies:
        copy.wait()


def step_call(spectrum, sea_mask, current, partners, source_map, coefs, drift_table, count, bands):
    local, rows, cols = spectrum.shape
    bins = local * count
    profiles = drift_table.shape[0]
    lats, lons = source_map.shape
    strip = cols // count
    each = strip // LANES
    pieces = cols // LANES
    vmem = pl.BlockSpec(memory_space=VMEM)
    hbm = pl.BlockSpec(memory_space=pl.ANY)
    dma = pltpu.SemaphoreType.DMA
    return pl.pallas_call(
        functools.partial(step_kernel, count, bands),
        out_shape=(
            jax.ShapeDtypeStruct(spectrum.shape, F32),
            jax.ShapeDtypeStruct((profiles, lats, lons), F32),
        ),
        in_specs=[hbm] + [vmem] * 6,
        out_specs=(hbm, hbm),
        scratch_shapes=[
            VMEM((local, rows, cols), F32),
            VMEM((rows, local, cols), F32),
            VMEM((2, pieces, local, TILE), F32),
            VMEM((2, each, bins, TILE), F32),
            VMEM((2, each, bins, TILE), F32),
            VMEM((2, pieces, local, TILE), F32),
            VMEM((bins, bins), jnp.bfloat16),
            VMEM((bins, bins), jnp.bfloat16),
            VMEM((bins, bins), jnp.bfloat16),
            VMEM((bins, 2 * each * TILE), jnp.bfloat16),
            VMEM((bins, 2 * each * TILE), jnp.bfloat16),
            VMEM((profiles, each * TILE), F32),
            VMEM((rows, cols), F32),
            VMEM((rows, cols), F32),
            VMEM((rows, cols), F32),
            VMEM((count, rows, TILE), F32),
            VMEM((2, local, cols), F32),
            VMEM((2, local, cols), F32),
            VMEM((2, local, cols), F32),
            VMEM((2, local, cols), F32),
            VMEM((rows + 2, strip + 16, profiles), F32),
            VMEM((lats, TILE), jnp.int32),
            VMEM((profiles, lats, lons), F32),
            dma((FORTH,)),
            dma((count,)),
            dma((count,)),
            dma((2,)),
            dma((2,)),
            dma((2, FORTH, count)),
            dma((2, FORTH, count)),
            dma((2, HOME, count)),
            dma((2, HOME, count)),
            dma((2, HOME)),
            dma((2, HOME)),
            dma((4,)),
            dma((4,)),
            dma((HOME,)),
            dma((lats // 8,)),
        ],
        compiler_params=pltpu.CompilerParams(
            collective_id=0, has_side_effects=True, vmem_limit_bytes=60 * 1024 * 1024
        ),
    )(spectrum, sea_mask, current, partners, source_map, coefs, drift_table)


def on_device_fast(spectrum, sea_mask, current, partner_plus, partner_minus, source_map):
    count = lax.axis_size("bins")
    bands = lax.axis_size("lat")
    along_x, along_y, strength, drift_table = fixed_tables()
    forth = np.maximum(along_y, 0.0) / 6.0
    back = np.minimum(along_y, 0.0) / 6.0
    coefs = np.stack(
        [
            along_x,
            forth,
            -6.0 * forth - 2.0 * back,
            3.0 * forth - 3.0 * back,
            2.0 * forth + 6.0 * back,
            -back,
            strength,
            np.zeros_like(forth),
        ],
        axis=1,
    ).astype(np.float32)
    second, stokes = step_call(
        spectrum,
        sea_mask,
        current.T,
        jnp.stack([partner_plus, partner_minus]),
        source_map.T,
        jnp.asarray(coefs),
        jnp.asarray(drift_table),
        count,
        bands,
    )
    lons, lats = source_map.shape
    return (second, jnp.swapaxes(stokes.reshape(2, LEV, lats, lons), 2, 3))


def on_device(spectrum, sea_mask, current, partner_plus, partner_minus, source_map):
    count = lax.axis_size("bins")
    bins, rows, cols = spectrum.shape
    bands = lax.axis_size("lat")
    lons, lats = source_map.shape
    strip = cols // count
    fits = (
        rows == 2 * GROUP
        and bins % (8 * FORTH) == 0
        and bins % (8 * HOME) == 0
        and cols % TILE == 0
        and strip * count == cols
        and strip % LANES == 0
        and strip <= TILE
        and bins * count % TILE == 0
        and lats == 2 * rows
        and lons == 2 * strip
        and lons <= TILE
        and count > 2
        and bands > 2
    )
    body = on_device_fast if fits else on_device_plain
    return body(spectrum, sea_mask, current, partner_plus, partner_minus, source_map)


def solution(mesh):
    return jax.shard_map(
        on_device,
        mesh=mesh,
        in_specs=(
            P("bins", "lat", None),
            P("lat", None),
            P("bins", "lat"),
            P(),
            P(),
            P("bins", "lat"),
        ),
        out_specs=(P("bins", "lat", None), P(None, None, "bins", "lat")),
        check_vma=False,
    )
```

```python
import functools
import math

import jax
import jax.numpy as jnp
import numpy as np
from jax import lax
from jax.experimental import pallas as pl
from jax.experimental.pallas import tpu as pltpu
from jax.sharding import PartitionSpec as P

NDIR = 36
NFREQ = 32
LEV = 64


HIGHEST = lax.Precision.HIGHEST


def extended(block, sides, width):
    for axis, dim in sides:
        count = lax.axis_size(axis)
        forward = [(i, i + 1) for i in range(count - 1)]
        backward = [(target, source) for source, target in forward]
        low = lax.ppermute(
            lax.slice_in_dim(block, block.shape[dim] - width, None, axis=dim), axis, forward
        )
        high = lax.ppermute(lax.slice_in_dim(block, 0, width, axis=dim), axis, backward)
        block = jnp.concatenate([low, block, high], axis=dim)
    return block


def bin_tables():
    dir_index = jnp.arange(NDIR, dtype=jnp.float32)
    freq_index = jnp.arange(NFREQ, dtype=jnp.float32)
    angles = 2.0 * math.pi * (dir_index + 0.5) / NDIR
    speeds = 0.12 + 0.25 * (NFREQ - 1 - freq_index) / (NFREQ - 1)
    along_x = jnp.repeat(speeds, NDIR) * jnp.tile(jnp.cos(angles), NFREQ)
    along_y = jnp.repeat(speeds, NDIR) * jnp.tile(jnp.sin(angles), NFREQ)
    strength = jnp.repeat(0.06 * (1.0 + freq_index / (NFREQ - 1)), NDIR)
    levels = jnp.arange(LEV, dtype=jnp.float32) + 0.5
    wavenumber = 0.02 * jnp.power(1.15, freq_index)
    decay = jnp.repeat(jnp.exp(-levels[:, None] * wavenumber[None, :]), NDIR, axis=1)
    amplitude = 2.0 / math.sqrt(NDIR * NFREQ)
    cosines = jnp.tile(jnp.cos(angles), NFREQ)
    sines = jnp.tile(jnp.sin(angles), NFREQ)
    drift_table = amplitude * jnp.concatenate(
        [decay * cosines[None, :], decay * sines[None, :]], axis=0
    )
    return (along_x, along_y, strength, drift_table)


def fixed_tables():
    dir_index = np.arange(NDIR, dtype=np.float32)
    freq_index = np.arange(NFREQ, dtype=np.float32)
    angles = 2.0 * math.pi * (dir_index + 0.5) / NDIR
    speeds = 0.12 + 0.25 * (NFREQ - 1 - freq_index) / (NFREQ - 1)
    along_x = np.repeat(speeds, NDIR) * np.tile(np.cos(angles), NFREQ)
    along_y = np.repeat(speeds, NDIR) * np.tile(np.sin(angles), NFREQ)
    strength = np.repeat(0.06 * (1.0 + freq_index / (NFREQ - 1)), NDIR)
    levels = np.arange(LEV, dtype=np.float32) + 0.5
    wavenumber = 0.02 * np.power(np.float32(1.15), freq_index)
    decay = np.repeat(np.exp(-levels[:, None] * wavenumber[None, :]), NDIR, axis=1)
    amplitude = 2.0 / math.sqrt(NDIR * NFREQ)
    cosines = np.tile(np.cos(angles), NFREQ)
    sines = np.tile(np.sin(angles), NFREQ)
    drift_table = amplitude * np.concatenate(
        [decay * cosines[None, :], decay * sines[None, :]], axis=0
    )
    tables = (along_x, along_y, strength, drift_table)
    return tuple(np.asarray(table, dtype=np.float32) for table in tables)


def cell_means(current_cells):
    lon_count = current_cells.shape[0] // 2
    lat_count = current_cells.shape[1] // 2
    return current_cells.reshape(lon_count, 2, lat_count, 2).mean(axis=(1, 3))


def face_fluxes(padded, velocity, dimension):
    face_count = padded.shape[dimension] - 3

    def section(low_edge):
        return lax.slice_in_dim(padded, low_edge, low_edge + face_count, axis=dimension)

    left_value = (-section(0) + 5.0 * section(1) + 2.0 * section(2)) / 6.0
    right_value = (2.0 * section(1) + 5.0 * section(2) - section(3)) / 6.0
    return jnp.maximum(velocity, 0.0) * left_value + jnp.minimum(velocity, 0.0) * right_value


def transport(padded_rows, zonal_flow, along_x, along_y, sea_cells):
    row_count = padded_rows.shape[1] - 4
    spectra = padded_rows[:, 2 : 2 + row_count, :]
    padded_cols = jnp.pad(spectra, ((0, 0), (0, 0), (2, 2)))
    zonal_padded = jnp.pad(zonal_flow, ((0, 0), (1, 1)))
    face_zonal = 0.5 * (zonal_padded[:, :-1] + zonal_padded[:, 1:])
    speed_x = along_x[:, None, None] + face_zonal[None, :, :]
    flux_x = face_fluxes(padded_cols, speed_x, 2)
    flux_y = face_fluxes(padded_rows, along_y[:, None, None], 1)
    change = flux_x[:, :, 1:] - flux_x[:, :, :-1] + flux_y[:, 1:, :] - flux_y[:, :-1, :]
    return sea_cells[None, :, :] * (spectra - change)


def spread_to_ocean(rim, source_map):
    row_count = rim.shape[1] - 2
    col_count = rim.shape[2] - 2
    result = jnp.zeros((rim.shape[0], 2 * col_count, 2 * row_count), jnp.float32)
    for offset in range(9):
        row_shift = offset // 3 - 1
        col_shift = offset % 3 - 1
        shifted = rim[
            :, 1 + row_shift : 1 + row_shift + row_count, 1 + col_shift : 1 + col_shift + col_count
        ]
        shifted = jnp.swapaxes(shifted, 1, 2)
        shifted = jnp.repeat(jnp.repeat(shifted, 2, axis=1), 2, axis=2)
        result = result + jnp.where(source_map[None, :, :] == offset, shifted, jnp.float32(0.0))
    return result


def on_device_plain(spectrum, sea_mask, current, partner_plus, partner_minus, source_map):
    along_x, along_y, strength, drift_table = bin_tables()
    bin_count = NDIR * NFREQ
    local_bins = spectrum.shape[0]
    first_bin = lax.axis_index("bins") * local_bins
    local_x = lax.dynamic_slice_in_dim(along_x, first_bin, local_bins)
    local_y = lax.dynamic_slice_in_dim(along_y, first_bin, local_bins)
    sea_cells = sea_mask.astype(jnp.float32)
    strip_flow = cell_means(current)
    zonal_flow = lax.all_gather(strip_flow, "bins", axis=0, tiled=True).T
    masked = spectrum * sea_cells[None, :, :]
    padded = extended(masked, (("lat", 1),), 2)
    after_first = transport(padded, zonal_flow, local_x, local_y, sea_cells)
    bin_ids = jnp.arange(bin_count, dtype=jnp.int32)
    plus_table = (partner_plus[:, None] == bin_ids[None, :]).astype(jnp.float32)
    minus_table = (partner_minus[:, None] == bin_ids[None, :]).astype(jnp.float32)
    contract_first = (((0,), (0,)), ((), ()))
    arrived = lax.all_to_all(after_first, "bins", split_axis=2, concat_axis=0, tiled=True)
    row_count = arrived.shape[1]
    col_count = arrived.shape[2]
    flat_rows = arrived.reshape(bin_count, row_count * col_count)
    plus_part = jnp.dot(plus_table, flat_rows, precision=HIGHEST)
    minus_part = jnp.dot(minus_table, flat_rows, precision=HIGHEST)
    source = strength[:, None] * (
        flat_rows * flat_rows * (plus_part + minus_part) - 2.0 * flat_rows * plus_part * minus_part
    )
    back = lax.dot_general(plus_table, source, contract_first, precision=HIGHEST) + lax.dot_general(
        minus_table, source, contract_first, precision=HIGHEST
    )
    middle = flat_rows + (source - 0.5 * back)
    drift_rows = jnp.dot(drift_table, middle, precision=HIGHEST)
    middle, drift_rows = (
        middle.reshape(bin_count, row_count, col_count),
        drift_rows.reshape(2 * LEV, row_count, col_count),
    )
    rim = extended(drift_rows, (("bins", 2), ("lat", 1)), 1)
    ocean = spread_to_ocean(rim, source_map)
    stokes = ocean.reshape(2, LEV, ocean.shape[1], ocean.shape[2])
    returned = lax.all_to_all(middle, "bins", split_axis=0, concat_axis=2, tiled=True)
    padded_again = extended(returned, (("lat", 1),), 2)
    second = transport(padded_again, zonal_flow, local_x, local_y, sea_cells)
    return (second, stokes)

MESH = pl.DeviceIdType.MESH
TILE = 128
GROUP = 8
LANES = TILE // GROUP
VMEM = pltpu.VMEM
LOADS = 3
STEPS = 9
LEAD = 2
FORTH = ((0, 1, 5, 9), (0, 4, 9))
HOME = ((0, 3, 6, 8, 9), (0, 3, 6, 9))
QUEUE = ((0, 0), (0, 1), (1, 0), (1, 1), (1, 2), (0, 2), (0, 3))
AHEAD = 2
F32 = jnp.float32


def row_groups(rows):
    edge = rows // 4
    inner = list(range(edge, rows - edge))
    return inner, list(range(edge)) + list(range(rows - edge, rows))


def turn_blocks(tiles):
    lane = lax.broadcasted_iota(jnp.int32, tiles[0].shape, 1) // LANES
    tiles = list(tiles)
    step = 1
    while step < GROUP:
        clear = lax.rem(lane // step, 2) == 0
        for i in range(GROUP):
            if i & step:
                continue
            upper, lower = tiles[i], tiles[i + step]
            tiles[i] = jnp.where(clear, upper, pltpu.roll(lower, step * LANES, 1))
            tiles[i + step] = jnp.where(clear, pltpu.roll(upper, TILE - step * LANES, 1), lower)
        step *= 2
    return tiles


def advect(get, wanted, coefs, face, half, mask):
    cols = face.shape[1]
    lane = lax.broadcasted_iota(jnp.int32, (8, cols), 1)
    at_first = lane == 0
    at_second = lane <= 1
    at_last = lane == cols - 1
    sixth = F32(1.0 / 6.0)
    coef = [jnp.broadcast_to(coefs[:, i : i + 1], (8, cols)) for i in range(6)]
    cache = {}

    def f(row):
        if row not in cache:
            cache[row] = get(row)
        return cache[row]

    results = []
    for row in wanted:
        c = f(row)
        m1 = jnp.where(at_first, 0.0, pltpu.roll(c, 1, 1))
        m2 = jnp.where(at_second, 0.0, pltpu.roll(c, 2, 1))
        p1 = jnp.where(at_last, 0.0, pltpu.roll(c, cols - 1, 1))
        speed = coef[0] + face[row : row + 1, :]
        ahead = speed > 0.0
        part = 3.0 * jnp.where(ahead, m1, c) - jnp.where(ahead, m2, p1)
        flux = (speed * sixth) * (part + 2.0 * (m1 + c))
        end_speed = coef[0] + half[row : row + 1, :]
        end = (end_speed * sixth) * jnp.where(end_speed > 0.0, 5.0 * c - m1, 2.0 * c)
        upper = jnp.where(at_last, end, pltpu.roll(flux, cols - 1, 1))
        along_y = (
            coef[1] * f(row - 2)
            + coef[2] * f(row - 1)
            + coef[3] * c
            + coef[4] * f(row + 1)
            + coef[5] * f(row + 2)
        )
        results.append(mask[row : row + 1, :] * (c - ((upper - flux) + along_y)))
    return results


def halves(value):
    high = value.astype(jnp.bfloat16)
    return high, (value - high.astype(F32)).astype(jnp.bfloat16)


def step_kernel(
    count,
    bands,
    x_ref,
    mask_hbm,
    current_hbm,
    plus_hbm,
    minus_hbm,
    source_hbm,
    table_hbm,
    drift_hbm,
    out_ref,
    stokes_ref,
    block,
    by_row,
    leaving,
    arrived,
    middle,
    returned,
    plus_table,
    minus_table,
    back_table,
    parts,
    source_parts,
    total,
    mask,
    half,
    face,
    strips,
    low_halo,
    high_halo,
    low_again,
    high_again,
    near,
    columns,
    chosen_map,
    ocean,
    coefs,
    table,
    drift_ref,
    mask_ref,
    current_ref,
    plus_ref,
    minus_ref,
    source_ref,
    load_sem,
    table_sem,
    strip_send,
    strip_recv,
    halo_send,
    halo_recv,
    in_send,
    in_recv,
    back_send,
    back_recv,
    again_send,
    again_recv,
    near_send,
    near_recv,
    out_sem,
    ocean_sem,
):
    me = lax.axis_index("bins")
    band = lax.axis_index("lat")
    local, rows, cols = block.shape
    bins = local * count
    strip = cols // count
    each = strip // LANES
    pieces = cols // LANES
    unit = local // STEPS
    tiles = bins // TILE
    width = each * TILE
    across = cols // TILE
    groups = row_groups(rows)
    below = lax.rem(band + bands - 1, bands)
    above = lax.rem(band + 1, bands)
    left = lax.rem(me + count - 1, count)
    right = lax.rem(me + 1, count)
    edges = (jnp.where(band > 0, F32(1.0), F32(0.0)), jnp.where(band < bands - 1, F32(1.0), F32(0.0)))

    def remote(src, dst, send_sem, recv_sem, peer, axis="bins"):
        return pltpu.make_async_remote_copy(
            src_ref=src,
            dst_ref=dst,
            send_sem=send_sem,
            recv_sem=recv_sem,
            device_id={axis: peer},
            device_id_type=MESH,
        )

    chunk_load = local // LOADS

    def load_copy(part):
        here = pl.ds(part * chunk_load, chunk_load)
        return pltpu.make_async_copy(x_ref.at[here], block.at[here], load_sem.at[part])

    first_bin = me * local
    own_bins = pl.ds(pl.multiple_of(first_bin, 8), local)
    table_copies = [
        pltpu.make_async_copy(src, dst, table_sem.at[i])
        for i, (src, dst) in enumerate(
            (
                (current_hbm, current_ref),
                (mask_hbm, mask_ref),
                (table_hbm.at[own_bins], coefs),
                (table_hbm, table),
                (drift_hbm, drift_ref),
                (plus_hbm, plus_ref),
                (minus_hbm, minus_ref),
                (source_hbm, source_ref),
            )
        )
    ]
    for copy in table_copies[:2]:
        copy.start()
    for part in range(LOADS):
        load_copy(part).start()

    near[...] = jnp.zeros_like(near)
    barrier = pltpu.get_barrier_semaphore()
    for step in range(1, count):
        pl.semaphore_signal(
            barrier,
            inc=1,
            device_id={"bins": lax.rem(me + step, count)},
            device_id_type=MESH,
        )
    for peer in (below, above):
        pl.semaphore_signal(barrier, inc=1, device_id={"lat": peer}, device_id_type=MESH)

    lons = current_ref.shape[1]
    for copy in table_copies[:2]:
        copy.wait()
    pairs = current_ref[pl.ds(0, rows, stride=2), :] + current_ref[pl.ds(1, rows, stride=2), :]
    fold = lax.broadcasted_iota(jnp.int32, (lons, TILE), 0) // 2
    fold = jnp.where(fold == lax.broadcasted_iota(jnp.int32, (lons, TILE), 1), F32(0.125), F32(0.0))
    strips[me] = jnp.dot(pairs, fold, precision=HIGHEST, preferred_element_type=F32)
    mask[...] = mask_ref[...].astype(F32)

    pl.semaphore_wait(barrier, count + 1)

    def strip_copy(step):
        peer = lax.rem(me + step, count)
        return remote(strips.at[me], strips.at[me], strip_send.at[step], strip_recv.at[step], peer)

    for step in range(1, count):
        strip_copy(step).start()

    for part in range(LOADS):
        load_copy(part).wait()

        def turn_step(i, carry, part=part):
            here = pl.ds(pl.multiple_of(part * chunk_load + i * 8, 8), 8)
            turned = pltpu.einshape("brl->rbl", block[here, :, :] * mask[...][None])
            for row in range(rows):
                by_row[row, here, :] = turned[row]
            return carry

        lax.fori_loop(0, chunk_load // 8, turn_step, 0)

    halo_copies = [
        remote(
            by_row.at[pl.ds(0, 2)], high_halo, halo_send.at[0], halo_recv.at[0], below, "lat"
        ),
        remote(
            by_row.at[pl.ds(rows - 2, 2)], low_halo, halo_send.at[1], halo_recv.at[1], above, "lat"
        ),
    ]
    for copy in halo_copies + table_copies[2:]:
        copy.start()
    table_copies[2].wait()
    for step in range(1, count):
        strip_copy(step).wait()
    spread = jnp.zeros((rows, cols), F32)
    rest = jnp.zeros((rows, cols - TILE), F32)
    for peer in range(count):
        piece = jnp.concatenate([strips[peer], rest], axis=1)
        spread = spread + (pltpu.roll(piece, peer * strip, 1) if peer else piece)
    half[...] = spread
    first_lane = lax.broadcasted_iota(jnp.int32, (rows, cols), 1) == 0
    face[...] = spread + jnp.where(first_lane, 0.0, pltpu.roll(spread, 1, 1))

    def fetch(here, low, high):
        def get(row):
            if row < 0:
                return edges[0] * low[row + 2, here, :]
            if row >= rows:
                return edges[1] * high[row - rows, here, :]
            return by_row[row, here, :]

        return get

    def coefs_at(start):
        return coefs[pl.ds(pl.multiple_of(start, 8), 8), :]

    def reach(cuts, part):
        return cuts[part] * unit, (cuts[part + 1] - cuts[part]) * unit

    def in_copy(h, part, step):
        peer = lax.rem(me + step, count)
        at, size = reach(FORTH[h], part)
        src = leaving.at[h, pl.ds(peer * each, each), pl.ds(at, size), :]
        dst = arrived.at[h, :, pl.ds(pl.multiple_of(first_bin + at, 8), size), :]
        if step == 0:
            return pltpu.make_async_copy(src, dst, in_recv.at[h, part, 0])
        return remote(src, dst, in_send.at[h, part, step], in_recv.at[h, part, step], peer)

    for h in range(2):
        if h == 1:
            for copy in halo_copies:
                copy.wait()

        def forth_turn(turn, carry, h=h):
            def forth_step(i, carry):
                start = turn * unit + i * 8
                here = pl.ds(pl.multiple_of(start, 8), 8)
                found = advect(
                    fetch(here, low_halo, high_halo),
                    groups[h],
                    coefs_at(start),
                    face[...],
                    half[...],
                    mask[...],
                )
                for t in range(across):
                    turned = turn_blocks([row[:, t * TILE : (t + 1) * TILE] for row in found])
                    for q in range(GROUP):
                        leaving[h, t * GROUP + q, here, :] = turned[q]
                return carry

            lax.fori_loop(0, unit // 8, forth_step, 0)
            for part, end in enumerate(FORTH[h][1:]):

                @pl.when(turn == end - 1)
                def _(part=part):
                    for step in range(1, count + 1):
                        in_copy(h, part, step % count).start()

            return carry

        lax.fori_loop(0, STEPS, forth_turn, 0)

    def table_step(tile, carry):
        here = pl.ds(pl.multiple_of(tile * TILE, TILE), TILE)
        along = lax.broadcasted_iota(jnp.int32, (TILE, bins), 1).astype(F32)
        down = (lax.broadcasted_iota(jnp.int32, (TILE, bins), 0) + tile * TILE).astype(F32)
        one = F32(1.0)
        zero = F32(0.0)
        back = jnp.zeros((TILE, bins), F32)
        for partner_ref, picks in ((plus_ref, plus_table), (minus_ref, minus_table)):
            column = jnp.broadcast_to(partner_ref[here][None, :], (TILE, TILE)).astype(F32).T
            column = jnp.concatenate([column] * tiles, axis=1)
            picks[here, :] = jnp.where(column == along, one, zero).astype(jnp.bfloat16)
            whole = partner_ref[...][None, :].astype(F32)
            back = back + jnp.where(whole == down, one, zero)
        back_table[here, :] = back.astype(jnp.bfloat16)
        return carry

    for copy in table_copies[3:]:
        copy.wait()
    lax.fori_loop(0, tiles, table_step, 0)

    def back_copy(h, part, step):
        peer = lax.rem(me + step, count)
        at, size = reach(HOME[h], part)
        src = middle.at[h, :, pl.ds(pl.multiple_of(peer * local + at, 8), size), :]
        dst = returned.at[h, pl.ds(me * each, each), pl.ds(at, size), :]
        if step == 0:
            return pltpu.make_async_copy(src, dst, back_recv.at[h, part, 0])
        return remote(src, dst, back_send.at[h, part, step], back_recv.at[h, part, step], peer)

    def send_back(at):
        for step in range(1, count + 1):
            back_copy(*QUEUE[at], step % count).start()

    def await_back(at):
        for step in range(count):
            back_copy(*QUEUE[at], step).wait()
        if at + AHEAD < len(QUEUE):
            send_back(at + AHEAD)

    def pick(table, here, value):
        both = jnp.dot(table[here, :], value[...], preferred_element_type=F32)
        return both[:, :width] + both[:, width:]

    def near_copy(slot):
        if slot == 0:
            src, dst, peer, axis = columns.at[0], columns.at[2], left, "bins"
        elif slot == 1:
            src, dst, peer, axis = columns.at[1], columns.at[3], right, "bins"
        elif slot == 2:
            src, dst, peer, axis = near.at[1], near.at[rows + 1], below, "lat"
        else:
            src, dst, peer, axis = near.at[rows], near.at[0], above, "lat"
        return remote(src, dst, near_send.at[slot], near_recv.at[slot], peer, axis)

    for h in range(2):
        for part in range(len(FORTH[h]) - 1):
            for step in range(count):
                in_copy(h, part, step).wait()

        def split_step(tile, carry, h=h):
            here = pl.ds(pl.multiple_of(tile * TILE, TILE), TILE)
            for g in range(each):
                upper, lower = halves(arrived[h, g, here, :])
                parts[here, g * TILE : (g + 1) * TILE] = upper
                parts[here, width + g * TILE : width + (g + 1) * TILE] = lower
            return carry

        lax.fori_loop(0, tiles, split_step, 0)

        def source_step(tile, carry, h=h):
            here = pl.ds(pl.multiple_of(tile * TILE, TILE), TILE)
            plus = pick(plus_table, here, parts)
            minus = pick(minus_table, here, parts)
            strength = table[here, 6:7]
            for g in range(each):
                lanes = slice(g * TILE, (g + 1) * TILE)
                own = arrived[h, g, here, :]
                p, m = plus[:, lanes], minus[:, lanes]
                source = strength * (own * own * (p + m) - 2.0 * own * p * m)
                upper, lower = halves(source)
                source_parts[here, lanes] = upper
                source_parts[here, width + g * TILE : width + (g + 1) * TILE] = lower
                middle[h, g, here, :] = own + source
            return carry

        lax.fori_loop(0, tiles, source_step, 0)
        total[...] = jnp.zeros_like(total)

        def back_step(tile, carry, h=h):
            here = pl.ds(pl.multiple_of(tile * TILE, TILE), TILE)
            back = pick(back_table, here, source_parts)
            done = []
            for g in range(each):
                value = middle[h, g, here, :] - 0.5 * back[:, g * TILE : (g + 1) * TILE]
                middle[h, g, here, :] = value
                done.append(value)
            total[...] += jnp.dot(
                drift_ref[:, here],
                jnp.concatenate(done, axis=1),
                precision=HIGHEST,
                preferred_element_type=F32,
            )
            return carry

        lax.fori_loop(0, tiles, back_step, 0)
        for g in range(each):
            points = total[:, g * TILE : (g + 1) * TILE].T
            for at, row in enumerate(groups[h]):
                near[1 + row, 8 + g * LANES : 8 + (g + 1) * LANES, :] = points[at * LANES : (at + 1) * LANES, :]
        if h == 1:
            for row in range(rows):
                columns[0, row : row + 1, :] = near[1 + row, 8:9, :]
                columns[1, row : row + 1, :] = near[1 + row, 7 + strip : 8 + strip, :]
            near_copy(0).start()
            near_copy(1).start()

        for at, (which, part) in enumerate(QUEUE[:AHEAD]):
            if which == h:
                send_back(at)

    await_back(0)
    near_copy(0).wait()
    near_copy(1).wait()
    side = (jnp.where(me > 0, F32(1.0), F32(0.0)), jnp.where(me < count - 1, F32(1.0), F32(0.0)))
    for row in range(rows):
        near[1 + row, 7:8, :] = columns[3, row : row + 1, :] * side[0]
        near[1 + row, 8 + strip : 9 + strip, :] = columns[2, row : row + 1, :] * side[1]
    near_copy(2).start()
    near_copy(3).start()

    chosen_map[...] = jnp.zeros_like(chosen_map)
    sources = source_ref[...]
    third = jnp.where(sources >= 3, 1, 0) + jnp.where(sources >= 6, 1, 0)
    extent = strip + 16
    column = lax.broadcasted_iota(jnp.int32, sources.shape, 1) // 2
    chosen_map[:, :lons] = third * extent + 7 + column + (sources - 3 * third)
    near_copy(2).wait()
    near_copy(3).wait()
    near[0] = near[0] * edges[0]
    near[rows + 1] = near[rows + 1] * edges[1]

    depth = 3 * extent
    profiles = near.shape[2]
    ocean_copies = []
    for octet in range(2 * rows // 8):
        found = []
        for row in range(octet * 4, octet * 4 + 4):
            window = near[row : row + 3].reshape(depth, profiles)
            down = lax.broadcasted_iota(jnp.int32, (depth, TILE), 0)
            chosen = [
                jnp.where(down == chosen_map[lat : lat + 1, :], F32(1.0), F32(0.0))
                for lat in (2 * row, 2 * row + 1)
            ]
            both = lax.dot_general(
                window,
                jnp.concatenate(chosen, axis=1),
                (((0,), (0,)), ((), ())),
                precision=HIGHEST,
                preferred_element_type=F32,
            )
            found += [both[:, :TILE], both[:, TILE:]]
        here = pl.ds(octet * 8, 8)
        ocean[:, here, :] = pltpu.einshape("ypl->pyl", jnp.stack(found))[:, :, :lons]
        copy = pltpu.make_async_copy(ocean.at[:, here, :], stokes_ref.at[:, here, :], ocean_sem.at[octet])
        copy.start()
        ocean_copies.append(copy)

    def again_copy(part, slot):
        here = pl.ds(pl.multiple_of(part * unit, 8), unit)
        if slot == 0:
            src, dst, peer = by_row.at[pl.ds(0, 2), here, :], high_again.at[:, here, :], below
        else:
            src, dst, peer = by_row.at[pl.ds(rows - 2, 2), here, :], low_again.at[:, here, :], above
        return remote(src, dst, again_send.at[slot, part], again_recv.at[slot, part], peer, "lat")

    def out_copy(part):
        here = pl.ds(part * unit, unit)
        return pltpu.make_async_copy(block.at[here], out_ref.at[here], out_sem.at[part])

    def unpack(h, turn):
        for at, (which, part) in enumerate(QUEUE):
            if which == h and at > 1:

                @pl.when(turn == HOME[h][part])
                def _(at=at):
                    await_back(at)

        def unpack_step(i, carry):
            here = pl.ds(pl.multiple_of(turn * unit + i * 8, 8), 8)
            for t in range(across):
                turned = turn_blocks([returned[h, t * GROUP + q, here, :] for q in range(GROUP)])
                for at, row in enumerate(groups[h]):
                    by_row[row, here, t * TILE : (t + 1) * TILE] = turned[at]
            return carry

        lax.fori_loop(0, unit // 8, unpack_step, 0)

    def home_part(turn, carry):
        @pl.when(turn < STEPS)
        def _():
            unpack(1, turn)
            again_copy(turn, 0).start()
            again_copy(turn, 1).start()

        @pl.when(turn >= LEAD)
        def _():
            part = turn - LEAD
            unpack(0, part)
            again_copy(part, 0).wait()
            again_copy(part, 1).wait()

            def home_step(i, carry):
                start = part * unit + i * 8
                here = pl.ds(pl.multiple_of(start, 8), 8)
                found = advect(
                    fetch(here, low_again, high_again),
                    list(range(rows)),
                    coefs_at(start),
                    face[...],
                    half[...],
                    mask[...],
                )
                block[here, :, :] = pltpu.einshape("rbl->brl", jnp.stack(found))
                return carry

            lax.fori_loop(0, unit // 8, home_step, 0)
            out_copy(part).start()

        return carry

    await_back(1)
    lax.fori_loop(0, STEPS + LEAD, home_part, 0)
    for part in range(STEPS):
        out_copy(part).wait()
    for copy in ocean_copies:
        copy.wait()


def step_call(spectrum, sea_mask, current, plus, minus, source_map, coefs, drift_table, count, bands):
    local, rows, cols = spectrum.shape
    bins = local * count
    profiles = drift_table.shape[0]
    lats, lons = source_map.shape
    strip = cols // count
    each = strip // LANES
    pieces = cols // LANES
    hbm = pl.BlockSpec(memory_space=pl.ANY)
    dma = pltpu.SemaphoreType.DMA
    forth = max(len(cuts) for cuts in FORTH) - 1
    home = max(len(cuts) for cuts in HOME) - 1
    return pl.pallas_call(
        functools.partial(step_kernel, count, bands),
        out_shape=(
            jax.ShapeDtypeStruct(spectrum.shape, F32),
            jax.ShapeDtypeStruct((profiles, lats, lons), F32),
        ),
        in_specs=[pl.BlockSpec(memory_space=pltpu.HBM)] * 8,
        out_specs=(hbm, hbm),
        scratch_shapes=[
            VMEM((local, rows, cols), F32),
            VMEM((rows, local, cols), F32),
            VMEM((2, pieces, local, TILE), F32),
            VMEM((2, each, bins, TILE), F32),
            VMEM((2, each, bins, TILE), F32),
            VMEM((2, pieces, local, TILE), F32),
            VMEM((bins, bins), jnp.bfloat16),
            VMEM((bins, bins), jnp.bfloat16),
            VMEM((bins, bins), jnp.bfloat16),
            VMEM((bins, 2 * each * TILE), jnp.bfloat16),
            VMEM((bins, 2 * each * TILE), jnp.bfloat16),
            VMEM((profiles, each * TILE), F32),
            VMEM((rows, cols), F32),
            VMEM((rows, cols), F32),
            VMEM((rows, cols), F32),
            VMEM((count, rows, TILE), F32),
            VMEM((2, local, cols), F32),
            VMEM((2, local, cols), F32),
            VMEM((2, local, cols), F32),
            VMEM((2, local, cols), F32),
            VMEM((rows + 2, strip + 16, profiles), F32),
            VMEM((4, rows, profiles), F32),
            VMEM((lats, TILE), jnp.int32),
            VMEM((profiles, lats, lons), F32),
            VMEM((local, coefs.shape[1]), F32),
            VMEM(coefs.shape, F32),
            VMEM(drift_table.shape, F32),
            VMEM(sea_mask.shape, jnp.int32),
            VMEM(current.shape, F32),
            VMEM(plus.shape, jnp.int32),
            VMEM(minus.shape, jnp.int32),
            VMEM(source_map.shape, jnp.int32),
            dma((LOADS,)),
            dma((8,)),
            dma((count,)),
            dma((count,)),
            dma((2,)),
            dma((2,)),
            dma((2, forth, count)),
            dma((2, forth, count)),
            dma((2, home, count)),
            dma((2, home, count)),
            dma((2, STEPS)),
            dma((2, STEPS)),
            dma((4,)),
            dma((4,)),
            dma((STEPS,)),
            dma((lats // 8,)),
        ],
        compiler_params=pltpu.CompilerParams(
            collective_id=0, has_side_effects=True, vmem_limit_bytes=58 * 1024 * 1024
        ),
    )(spectrum, sea_mask, current, plus, minus, source_map, coefs, drift_table)


def on_device_fast(spectrum, sea_mask, current, partner_plus, partner_minus, source_map):
    count = lax.axis_size("bins")
    bands = lax.axis_size("lat")
    along_x, along_y, strength, drift_table = fixed_tables()
    forth = np.maximum(along_y, 0.0) / 6.0
    back = np.minimum(along_y, 0.0) / 6.0
    coefs = np.stack(
        [
            along_x,
            forth,
            -6.0 * forth - 2.0 * back,
            3.0 * forth - 3.0 * back,
            2.0 * forth + 6.0 * back,
            -back,
            strength,
            np.zeros_like(forth),
        ],
        axis=1,
    ).astype(np.float32)
    second, stokes = step_call(
        spectrum,
        sea_mask,
        current.T,
        partner_plus,
        partner_minus,
        source_map.T,
        jnp.asarray(coefs),
        jnp.asarray(drift_table),
        count,
        bands,
    )
    lons, lats = source_map.shape
    return (second, jnp.swapaxes(stokes.reshape(2, LEV, lats, lons), 2, 3))


def on_device(spectrum, sea_mask, current, partner_plus, partner_minus, source_map):
    count = lax.axis_size("bins")
    bins, rows, cols = spectrum.shape
    bands = lax.axis_size("lat")
    lons, lats = source_map.shape
    strip = cols // count
    fits = (
        rows == 2 * GROUP
        and bins % (8 * STEPS) == 0
        and bins % (8 * LOADS) == 0
        and cols % TILE == 0
        and strip * count == cols
        and strip % LANES == 0
        and strip <= TILE
        and bins * count % TILE == 0
        and lats == 2 * rows
        and lons == 2 * strip
        and lons <= TILE
        and count > 2
        and bands > 2
    )
    body = on_device_fast if fits else on_device_plain
    return body(spectrum, sea_mask, current, partner_plus, partner_minus, source_map)


def solution(mesh):
    return jax.shard_map(
        on_device,
        mesh=mesh,
        in_specs=(
            P("bins", "lat", None),
            P("lat", None),
            P("bins", "lat"),
            P(),
            P(),
            P("bins", "lat"),
        ),
        out_specs=(P("bins", "lat", None), P(None, None, "bins", "lat")),
        check_vma=False,
    )
```

```python
import functools
import math

import jax
import jax.numpy as jnp
import numpy as np
from jax import lax
from jax.experimental import pallas as pl
from jax.experimental.pallas import tpu as pltpu
from jax.sharding import PartitionSpec as P

NDIR = 36
NFREQ = 32
LEV = 64


HIGHEST = lax.Precision.HIGHEST


def extended(block, sides, width):
    for axis, dim in sides:
        count = lax.axis_size(axis)
        forward = [(i, i + 1) for i in range(count - 1)]
        backward = [(target, source) for source, target in forward]
        low = lax.ppermute(
            lax.slice_in_dim(block, block.shape[dim] - width, None, axis=dim), axis, forward
        )
        high = lax.ppermute(lax.slice_in_dim(block, 0, width, axis=dim), axis, backward)
        block = jnp.concatenate([low, block, high], axis=dim)
    return block


def bin_tables():
    dir_index = jnp.arange(NDIR, dtype=jnp.float32)
    freq_index = jnp.arange(NFREQ, dtype=jnp.float32)
    angles = 2.0 * math.pi * (dir_index + 0.5) / NDIR
    speeds = 0.12 + 0.25 * (NFREQ - 1 - freq_index) / (NFREQ - 1)
    along_x = jnp.repeat(speeds, NDIR) * jnp.tile(jnp.cos(angles), NFREQ)
    along_y = jnp.repeat(speeds, NDIR) * jnp.tile(jnp.sin(angles), NFREQ)
    strength = jnp.repeat(0.06 * (1.0 + freq_index / (NFREQ - 1)), NDIR)
    levels = jnp.arange(LEV, dtype=jnp.float32) + 0.5
    wavenumber = 0.02 * jnp.power(1.15, freq_index)
    decay = jnp.repeat(jnp.exp(-levels[:, None] * wavenumber[None, :]), NDIR, axis=1)
    amplitude = 2.0 / math.sqrt(NDIR * NFREQ)
    cosines = jnp.tile(jnp.cos(angles), NFREQ)
    sines = jnp.tile(jnp.sin(angles), NFREQ)
    drift_table = amplitude * jnp.concatenate(
        [decay * cosines[None, :], decay * sines[None, :]], axis=0
    )
    return (along_x, along_y, strength, drift_table)


def fixed_tables():
    dir_index = np.arange(NDIR, dtype=np.float32)
    freq_index = np.arange(NFREQ, dtype=np.float32)
    angles = 2.0 * math.pi * (dir_index + 0.5) / NDIR
    speeds = 0.12 + 0.25 * (NFREQ - 1 - freq_index) / (NFREQ - 1)
    along_x = np.repeat(speeds, NDIR) * np.tile(np.cos(angles), NFREQ)
    along_y = np.repeat(speeds, NDIR) * np.tile(np.sin(angles), NFREQ)
    strength = np.repeat(0.06 * (1.0 + freq_index / (NFREQ - 1)), NDIR)
    levels = np.arange(LEV, dtype=np.float32) + 0.5
    wavenumber = 0.02 * np.power(np.float32(1.15), freq_index)
    decay = np.repeat(np.exp(-levels[:, None] * wavenumber[None, :]), NDIR, axis=1)
    amplitude = 2.0 / math.sqrt(NDIR * NFREQ)
    cosines = np.tile(np.cos(angles), NFREQ)
    sines = np.tile(np.sin(angles), NFREQ)
    drift_table = amplitude * np.concatenate(
        [decay * cosines[None, :], decay * sines[None, :]], axis=0
    )
    tables = (along_x, along_y, strength, drift_table)
    return tuple(np.asarray(table, dtype=np.float32) for table in tables)


def cell_means(current_cells):
    lon_count = current_cells.shape[0] // 2
    lat_count = current_cells.shape[1] // 2
    return current_cells.reshape(lon_count, 2, lat_count, 2).mean(axis=(1, 3))


def face_fluxes(padded, velocity, dimension):
    face_count = padded.shape[dimension] - 3

    def section(low_edge):
        return lax.slice_in_dim(padded, low_edge, low_edge + face_count, axis=dimension)

    left_value = (-section(0) + 5.0 * section(1) + 2.0 * section(2)) / 6.0
    right_value = (2.0 * section(1) + 5.0 * section(2) - section(3)) / 6.0
    return jnp.maximum(velocity, 0.0) * left_value + jnp.minimum(velocity, 0.0) * right_value


def transport(padded_rows, zonal_flow, along_x, along_y, sea_cells):
    row_count = padded_rows.shape[1] - 4
    spectra = padded_rows[:, 2 : 2 + row_count, :]
    padded_cols = jnp.pad(spectra, ((0, 0), (0, 0), (2, 2)))
    zonal_padded = jnp.pad(zonal_flow, ((0, 0), (1, 1)))
    face_zonal = 0.5 * (zonal_padded[:, :-1] + zonal_padded[:, 1:])
    speed_x = along_x[:, None, None] + face_zonal[None, :, :]
    flux_x = face_fluxes(padded_cols, speed_x, 2)
    flux_y = face_fluxes(padded_rows, along_y[:, None, None], 1)
    change = flux_x[:, :, 1:] - flux_x[:, :, :-1] + flux_y[:, 1:, :] - flux_y[:, :-1, :]
    return sea_cells[None, :, :] * (spectra - change)


def spread_to_ocean(rim, source_map):
    row_count = rim.shape[1] - 2
    col_count = rim.shape[2] - 2
    result = jnp.zeros((rim.shape[0], 2 * col_count, 2 * row_count), jnp.float32)
    for offset in range(9):
        row_shift = offset // 3 - 1
        col_shift = offset % 3 - 1
        shifted = rim[
            :, 1 + row_shift : 1 + row_shift + row_count, 1 + col_shift : 1 + col_shift + col_count
        ]
        shifted = jnp.swapaxes(shifted, 1, 2)
        shifted = jnp.repeat(jnp.repeat(shifted, 2, axis=1), 2, axis=2)
        result = result + jnp.where(source_map[None, :, :] == offset, shifted, jnp.float32(0.0))
    return result


def on_device_plain(spectrum, sea_mask, current, partner_plus, partner_minus, source_map):
    along_x, along_y, strength, drift_table = bin_tables()
    bin_count = NDIR * NFREQ
    local_bins = spectrum.shape[0]
    first_bin = lax.axis_index("bins") * local_bins
    local_x = lax.dynamic_slice_in_dim(along_x, first_bin, local_bins)
    local_y = lax.dynamic_slice_in_dim(along_y, first_bin, local_bins)
    sea_cells = sea_mask.astype(jnp.float32)
    strip_flow = cell_means(current)
    zonal_flow = lax.all_gather(strip_flow, "bins", axis=0, tiled=True).T
    masked = spectrum * sea_cells[None, :, :]
    padded = extended(masked, (("lat", 1),), 2)
    after_first = transport(padded, zonal_flow, local_x, local_y, sea_cells)
    bin_ids = jnp.arange(bin_count, dtype=jnp.int32)
    plus_table = (partner_plus[:, None] == bin_ids[None, :]).astype(jnp.float32)
    minus_table = (partner_minus[:, None] == bin_ids[None, :]).astype(jnp.float32)
    contract_first = (((0,), (0,)), ((), ()))
    arrived = lax.all_to_all(after_first, "bins", split_axis=2, concat_axis=0, tiled=True)
    row_count = arrived.shape[1]
    col_count = arrived.shape[2]
    flat_rows = arrived.reshape(bin_count, row_count * col_count)
    plus_part = jnp.dot(plus_table, flat_rows, precision=HIGHEST)
    minus_part = jnp.dot(minus_table, flat_rows, precision=HIGHEST)
    source = strength[:, None] * (
        flat_rows * flat_rows * (plus_part + minus_part) - 2.0 * flat_rows * plus_part * minus_part
    )
    back = lax.dot_general(plus_table, source, contract_first, precision=HIGHEST) + lax.dot_general(
        minus_table, source, contract_first, precision=HIGHEST
    )
    middle = flat_rows + (source - 0.5 * back)
    drift_rows = jnp.dot(drift_table, middle, precision=HIGHEST)
    middle, drift_rows = (
        middle.reshape(bin_count, row_count, col_count),
        drift_rows.reshape(2 * LEV, row_count, col_count),
    )
    rim = extended(drift_rows, (("bins", 2), ("lat", 1)), 1)
    ocean = spread_to_ocean(rim, source_map)
    stokes = ocean.reshape(2, LEV, ocean.shape[1], ocean.shape[2])
    returned = lax.all_to_all(middle, "bins", split_axis=0, concat_axis=2, tiled=True)
    padded_again = extended(returned, (("lat", 1),), 2)
    second = transport(padded_again, zonal_flow, local_x, local_y, sea_cells)
    return (second, stokes)

MESH = pl.DeviceIdType.MESH
TILE = 128
GROUP = 8
LANES = TILE // GROUP
VMEM = pltpu.VMEM
LOADS = 3
STEPS = 9
LEAD = 2
FORTH = ((0, 1, 5, 9), (0, 4, 9))
HOME = ((0, 3, 6, 8, 9), (0, 3, 6, 9))
LAST = 1
PLANES = 2
QUEUE = ((0, 0), (0, 1), (1, 0), (1, 1), (1, 2), (0, 2), (0, 3))
AHEAD = 2


def order(count):
    return list(range(count // 2, count)) + list(range(1, count // 2)) + [0]
F32 = jnp.float32


def row_groups(rows):
    edge = rows // 4
    inner = list(range(edge, rows - edge))
    return inner, list(range(edge)) + list(range(rows - edge, rows))


def turn_blocks(tiles):
    lane = lax.broadcasted_iota(jnp.int32, tiles[0].shape, 1) // LANES
    tiles = list(tiles)
    step = 1
    while step < GROUP:
        clear = lax.rem(lane // step, 2) == 0
        for i in range(GROUP):
            if i & step:
                continue
            upper, lower = tiles[i], tiles[i + step]
            tiles[i] = jnp.where(clear, upper, pltpu.roll(lower, step * LANES, 1))
            tiles[i + step] = jnp.where(clear, pltpu.roll(upper, TILE - step * LANES, 1), lower)
        step *= 2
    return tiles


def advect(get, wanted, coefs, face_ref, half_ref, mask_ref, put):
    cols = face_ref.shape[1]
    across = cols // TILE
    lane = lax.broadcasted_iota(jnp.int32, (8, TILE), 1)
    at_first = lane == 0
    at_second = lane <= 1
    at_last = lane == TILE - 1
    coef = [jnp.broadcast_to(coefs[:, i : i + 1], (8, TILE)) for i in range(6)]
    for row in wanted:
        c = [get(row, t) for t in range(across)]
        one = [pltpu.roll(value, 1, 1) for value in c]
        two = [pltpu.roll(value, 2, 1) for value in c]
        back = [pltpu.roll(value, TILE - 1, 1) for value in c]
        flux = []
        for t in range(across):
            lanes = slice(t * TILE, (t + 1) * TILE)
            m1 = jnp.where(at_first, one[t - 1] if t else 0.0, one[t])
            m2 = jnp.where(at_second, two[t - 1] if t else 0.0, two[t])
            p1 = jnp.where(at_last, back[t + 1] if t + 1 < across else 0.0, back[t])
            speed = coef[0] + face_ref[row : row + 1, lanes]
            ahead = speed > 0.0
            part = 3.0 * jnp.where(ahead, m1, c[t]) - jnp.where(ahead, m2, p1)
            flux.append(speed * (part + 2.0 * (m1 + c[t])))
            if t + 1 == across:
                end_speed = coef[0] + half_ref[row : row + 1, lanes]
                end = end_speed * jnp.where(end_speed > 0.0, 5.0 * c[t] - m1, 2.0 * c[t])
        shifted = [pltpu.roll(value, TILE - 1, 1) for value in flux]
        for t in range(across):
            lanes = slice(t * TILE, (t + 1) * TILE)
            upper = jnp.where(at_last, shifted[t + 1] if t + 1 < across else end, shifted[t])
            along_y = (
                coef[1] * get(row - 2, t)
                + coef[2] * get(row - 1, t)
                + coef[3] * c[t]
                + coef[4] * get(row + 1, t)
                + coef[5] * get(row + 2, t)
            )
            put(row, t, mask_ref[row : row + 1, lanes] * (c[t] - ((upper - flux[t]) + along_y)))


def halves(value):
    high = value.astype(jnp.bfloat16)
    return high, (value - high.astype(F32)).astype(jnp.bfloat16)


def step_kernel(
    count,
    bands,
    x_ref,
    mask_hbm,
    current_hbm,
    plus_hbm,
    minus_hbm,
    source_hbm,
    table_hbm,
    drift_hbm,
    out_ref,
    stokes_ref,
    rows_out,
    low_out,
    high_out,
    fields_out,
    coefs_out,
    block,
    by_row,
    leaving,
    arrived,
    middle,
    returned,
    plus_table,
    minus_table,
    back_table,
    parts,
    source_parts,
    total,
    mask,
    half,
    face,
    strips,
    low_halo,
    high_halo,
    low_again,
    high_again,
    near,
    columns,
    chosen_map,
    ocean,
    coefs,
    table,
    drift_ref,
    mask_ref,
    current_ref,
    plus_ref,
    minus_ref,
    source_ref,
    load_sem,
    table_sem,
    strip_send,
    strip_recv,
    halo_send,
    halo_recv,
    in_send,
    in_recv,
    back_send,
    back_recv,
    again_send,
    again_recv,
    near_send,
    near_recv,
    out_sem,
    ocean_sem,
    rows_sem,
    fields_sem,
):
    me = lax.axis_index("bins")
    band = lax.axis_index("lat")
    rows, local, cols = by_row.shape
    bins = local * count
    strip = cols // count
    each = strip // LANES
    pieces = cols // LANES
    unit = local // STEPS
    tiles = bins // TILE
    width = each * TILE
    across = cols // TILE
    groups = row_groups(rows)
    below = lax.rem(band + bands - 1, bands)
    above = lax.rem(band + 1, bands)
    left = lax.rem(me + count - 1, count)
    right = lax.rem(me + 1, count)
    edges = (jnp.where(band > 0, F32(1.0), F32(0.0)), jnp.where(band < bands - 1, F32(1.0), F32(0.0)))

    def remote(src, dst, send_sem, recv_sem, peer, axis="bins"):
        return pltpu.make_async_remote_copy(
            src_ref=src,
            dst_ref=dst,
            send_sem=send_sem,
            recv_sem=recv_sem,
            device_id={axis: peer},
            device_id_type=MESH,
        )

    chunk_load = local // LOADS

    def load_copy(part, t):
        here = pl.ds(part * chunk_load * rows, chunk_load * rows)
        return pltpu.make_async_copy(
            x_ref.at[here, pl.ds(t * TILE, TILE)], block.at[t, here, :], load_sem.at[part, t]
        )

    first_bin = me * local
    own_bins = pl.ds(pl.multiple_of(first_bin, 8), local)
    table_copies = [
        pltpu.make_async_copy(src, dst, table_sem.at[i])
        for i, (src, dst) in enumerate(
            (
                (current_hbm, current_ref),
                (mask_hbm, mask_ref),
                (table_hbm.at[own_bins], coefs),
                (table_hbm, table),
                (drift_hbm, drift_ref),
                (plus_hbm, plus_ref),
                (minus_hbm, minus_ref),
                (source_hbm, source_ref),
            )
        )
    ]
    for copy in table_copies[:2]:
        copy.start()
    for part in range(LOADS):
        for t in range(across):
            load_copy(part, t).start()

    near[...] = jnp.zeros_like(near)
    barrier = pltpu.get_barrier_semaphore()
    for step in range(1, count):
        pl.semaphore_signal(
            barrier,
            inc=1,
            device_id={"bins": lax.rem(me + step, count)},
            device_id_type=MESH,
        )
    for peer in (below, above):
        pl.semaphore_signal(barrier, inc=1, device_id={"lat": peer}, device_id_type=MESH)

    lons = current_ref.shape[1]
    for copy in table_copies[:2]:
        copy.wait()
    pairs = current_ref[pl.ds(0, rows, stride=2), :] + current_ref[pl.ds(1, rows, stride=2), :]
    fold = lax.broadcasted_iota(jnp.int32, (lons, TILE), 0) // 2
    fold = jnp.where(fold == lax.broadcasted_iota(jnp.int32, (lons, TILE), 1), F32(0.125), F32(0.0))
    strips[me] = jnp.dot(pairs, fold, precision=HIGHEST, preferred_element_type=F32)
    mask[...] = mask_ref[...].astype(F32)

    pl.semaphore_wait(barrier, count + 1)

    def strip_copy(step):
        peer = lax.rem(me + step, count)
        return remote(strips.at[me], strips.at[me], strip_send.at[step], strip_recv.at[step], peer)

    for step in range(1, count):
        strip_copy(step).start()

    for part in range(LOADS):
        for t in range(across):
            load_copy(part, t).wait()

        def turn_step(i, carry, part=part):
            here = pl.ds(pl.multiple_of(part * chunk_load + i * 8, 8), 8)
            start = (part * chunk_load + i * 8) * rows
            for row in range(rows):
                there = pl.ds(start + row, 8, stride=rows)
                for t in range(across):
                    lanes = slice(t * TILE, (t + 1) * TILE)
                    by_row[row, here, lanes] = block[t, there, :] * mask[row : row + 1, lanes]
            return carry

        lax.fori_loop(0, chunk_load // 8, turn_step, 0)

    halo_copies = [
        remote(
            by_row.at[pl.ds(0, 2)], high_halo, halo_send.at[0], halo_recv.at[0], below, "lat"
        ),
        remote(
            by_row.at[pl.ds(rows - 2, 2)], low_halo, halo_send.at[1], halo_recv.at[1], above, "lat"
        ),
    ]
    for copy in halo_copies + table_copies[2:]:
        copy.start()
    table_copies[2].wait()
    for step in range(1, count):
        strip_copy(step).wait()
    spread = jnp.zeros((rows, cols), F32)
    rest = jnp.zeros((rows, cols - TILE), F32)
    for peer in range(count):
        piece = jnp.concatenate([strips[peer], rest], axis=1)
        spread = spread + (pltpu.roll(piece, peer * strip, 1) if peer else piece)
    spread = spread * F32(1.0 / 6.0)
    half[...] = spread
    first_lane = lax.broadcasted_iota(jnp.int32, (rows, cols), 1) == 0
    face[...] = spread + jnp.where(first_lane, 0.0, pltpu.roll(spread, 1, 1))
    field_copies = [
        pltpu.make_async_copy(src, dst, fields_sem.at[i])
        for i, (src, dst) in enumerate(
            (
                (face, fields_out.at[0]),
                (half, fields_out.at[1]),
                (mask, fields_out.at[2]),
                (coefs, coefs_out),
            )
        )
    ]

    def fetch(here, low, high):
        def get(row, t):
            lanes = slice(t * TILE, (t + 1) * TILE)
            if row < 0:
                return edges[0] * low[row + 2, here, lanes]
            if row >= rows:
                return edges[1] * high[row - rows, here, lanes]
            return by_row[row, here, lanes]

        return get

    def coefs_at(start):
        return coefs[pl.ds(pl.multiple_of(start, 8), 8), :]

    def flip(step):
        peer = me
        weight = 1
        while weight < count:
            if step & weight:
                peer = peer + weight - 2 * weight * lax.rem(me // weight, 2)
            weight *= 2
        return peer

    def reach(cuts, part):
        return cuts[part] * unit, (cuts[part + 1] - cuts[part]) * unit

    def in_copy(h, part, step):
        peer = flip(step)
        at, size = reach(FORTH[h], part)
        src = leaving.at[h, pl.ds(peer * each, each), pl.ds(at, size), :]
        dst = arrived.at[h, :, pl.ds(pl.multiple_of(first_bin + at, 8), size), :]
        if step == 0:
            return pltpu.make_async_copy(src, dst, in_recv.at[h, part, 0])
        return remote(src, dst, in_send.at[h, part, step], in_recv.at[h, part, step], peer)

    for h in range(2):
        if h == 1:
            for copy in halo_copies:
                copy.wait()

        def forth_turn(turn, carry, h=h):
            def forth_step(i, carry):
                start = turn * unit + i * 8
                here = pl.ds(pl.multiple_of(start, 8), 8)
                found = {}
                advect(
                    fetch(here, low_halo, high_halo),
                    groups[h],
                    coefs_at(start),
                    face,
                    half,
                    mask,
                    lambda row, t, value: found.update({(row, t): value}),
                )
                for t in range(across):
                    turned = turn_blocks([found[row, t] for row in groups[h]])
                    for q in range(GROUP):
                        leaving[h, t * GROUP + q, here, :] = turned[q]
                return carry

            lax.fori_loop(0, unit // 8, forth_step, 0)
            for part, end in enumerate(FORTH[h][1:]):

                @pl.when(turn == end - 1)
                def _(part=part):
                    for step in order(count):
                        in_copy(h, part, step).start()

            return carry

        lax.fori_loop(0, STEPS, forth_turn, 0)

    def table_step(tile, carry):
        here = pl.ds(pl.multiple_of(tile * TILE, TILE), TILE)
        along = lax.broadcasted_iota(jnp.int32, (TILE, bins), 1).astype(F32)
        down = (lax.broadcasted_iota(jnp.int32, (TILE, bins), 0) + tile * TILE).astype(F32)
        one = F32(1.0)
        zero = F32(0.0)
        back = jnp.zeros((TILE, bins), F32)
        for partner_ref, picks in ((plus_ref, plus_table), (minus_ref, minus_table)):
            column = jnp.broadcast_to(partner_ref[here][None, :], (TILE, TILE)).astype(F32).T
            column = jnp.concatenate([column] * tiles, axis=1)
            picks[here, :] = jnp.where(column == along, one, zero).astype(jnp.bfloat16)
            whole = partner_ref[...][None, :].astype(F32)
            back = back + jnp.where(whole == down, one, zero)
        back_table[here, :] = back.astype(jnp.bfloat16)
        return carry

    for copy in field_copies:
        copy.start()
    for copy in table_copies[3:]:
        copy.wait()
    lax.fori_loop(0, tiles, table_step, 0)

    def back_copy(h, part, step):
        peer = flip(step)
        at, size = reach(HOME[h], part)
        src = middle.at[h, :, pl.ds(pl.multiple_of(peer * local + at, 8), size), :]
        dst = returned.at[h, pl.ds(me * each, each), pl.ds(at, size), :]
        if step == 0:
            return pltpu.make_async_copy(src, dst, back_recv.at[h, part, 0])
        return remote(src, dst, back_send.at[h, part, step], back_recv.at[h, part, step], peer)

    def send_back(at):
        for step in order(count):
            back_copy(*QUEUE[at], step).start()

    def await_back(at):
        for step in range(count):
            back_copy(*QUEUE[at], step).wait()
        if at + AHEAD < len(QUEUE):
            send_back(at + AHEAD)

    def pick(table, here, value):
        both = jnp.dot(table[here, :], value[...], preferred_element_type=F32)
        return both[:, :width] + both[:, width:]

    def near_copy(slot):
        if slot == 0:
            src, dst, peer, axis = columns.at[0], columns.at[2], left, "bins"
        elif slot == 1:
            src, dst, peer, axis = columns.at[1], columns.at[3], right, "bins"
        elif slot == 2:
            src, dst, peer, axis = near.at[1], near.at[rows + 1], below, "lat"
        else:
            src, dst, peer, axis = near.at[rows], near.at[0], above, "lat"
        return remote(src, dst, near_send.at[slot], near_recv.at[slot], peer, axis)

    for h in range(2):
        for part in range(len(FORTH[h]) - 1):
            for step in range(count):
                in_copy(h, part, step).wait()

        def split_step(tile, carry, h=h):
            here = pl.ds(pl.multiple_of(tile * TILE, TILE), TILE)
            for g in range(each):
                upper, lower = halves(arrived[h, g, here, :])
                parts[here, g * TILE : (g + 1) * TILE] = upper
                parts[here, width + g * TILE : width + (g + 1) * TILE] = lower
            return carry

        lax.fori_loop(0, tiles, split_step, 0)

        def source_step(tile, carry, h=h):
            here = pl.ds(pl.multiple_of(tile * TILE, TILE), TILE)
            plus = pick(plus_table, here, parts)
            minus = pick(minus_table, here, parts)
            strength = table[here, 6:7]
            for g in range(each):
                lanes = slice(g * TILE, (g + 1) * TILE)
                own = arrived[h, g, here, :]
                p, m = plus[:, lanes], minus[:, lanes]
                source = strength * (own * own * (p + m) - 2.0 * own * p * m)
                upper, lower = halves(source)
                source_parts[here, lanes] = upper
                source_parts[here, width + g * TILE : width + (g + 1) * TILE] = lower
                middle[h, g, here, :] = own + source
            return carry

        lax.fori_loop(0, tiles, source_step, 0)
        total[...] = jnp.zeros_like(total)

        def back_step(tile, carry, h=h):
            here = pl.ds(pl.multiple_of(tile * TILE, TILE), TILE)
            back = pick(back_table, here, source_parts)
            done = []
            for g in range(each):
                value = middle[h, g, here, :] - 0.5 * back[:, g * TILE : (g + 1) * TILE]
                middle[h, g, here, :] = value
                done.append(value)
            total[...] += jnp.dot(
                drift_ref[:, here],
                jnp.concatenate(done, axis=1),
                precision=HIGHEST,
                preferred_element_type=F32,
            )
            return carry

        lax.fori_loop(0, tiles, back_step, 0)
        for g in range(each):
            points = total[:, g * TILE : (g + 1) * TILE].T
            for at, row in enumerate(groups[h]):
                near[1 + row, 8 + g * LANES : 8 + (g + 1) * LANES, :] = points[at * LANES : (at + 1) * LANES, :]
        if h == 1:
            for row in range(rows):
                columns[0, row : row + 1, :] = near[1 + row, 8:9, :]
                columns[1, row : row + 1, :] = near[1 + row, 7 + strip : 8 + strip, :]
            near_copy(0).start()
            near_copy(1).start()

        for at, (which, part) in enumerate(QUEUE[:AHEAD]):
            if which == h:
                send_back(at)

    await_back(0)
    near_copy(0).wait()
    near_copy(1).wait()
    side = (jnp.where(me > 0, F32(1.0), F32(0.0)), jnp.where(me < count - 1, F32(1.0), F32(0.0)))
    for row in range(rows):
        near[1 + row, 7:8, :] = columns[3, row : row + 1, :] * side[0]
        near[1 + row, 8 + strip : 9 + strip, :] = columns[2, row : row + 1, :] * side[1]
    near_copy(2).start()
    near_copy(3).start()

    chosen_map[...] = jnp.zeros_like(chosen_map)
    sources = source_ref[...]
    third = jnp.where(sources >= 3, 1, 0) + jnp.where(sources >= 6, 1, 0)
    extent = strip + 16
    column = lax.broadcasted_iota(jnp.int32, sources.shape, 1) // 2
    chosen_map[:, :lons] = third * extent + 7 + column + (sources - 3 * third)
    near_copy(2).wait()
    near_copy(3).wait()
    near[0] = near[0] * edges[0]
    near[rows + 1] = near[rows + 1] * edges[1]

    depth = 3 * extent
    profiles = near.shape[2]
    ocean_copies = []
    for octet in range(2 * rows // 8):
        found = []
        for row in range(octet * 4, octet * 4 + 4):
            window = near[row : row + 3].reshape(depth, profiles)
            down = lax.broadcasted_iota(jnp.int32, (depth, TILE), 0)
            chosen = [
                jnp.where(down == chosen_map[lat : lat + 1, :], F32(1.0), F32(0.0))
                for lat in (2 * row, 2 * row + 1)
            ]
            both = lax.dot_general(
                window,
                jnp.concatenate(chosen, axis=1),
                (((0,), (0,)), ((), ())),
                precision=HIGHEST,
                preferred_element_type=F32,
            )
            found += [both[:, :TILE], both[:, TILE:]]
        here = pl.ds(octet * 8, 8)
        ocean[:, here, :] = pltpu.einshape("ypl->pyl", jnp.stack(found))[:, :, :lons]
        copy = pltpu.make_async_copy(ocean.at[:, here, :], stokes_ref.at[:, here, :], ocean_sem.at[octet])
        copy.start()
        ocean_copies.append(copy)

    def again_copy(part, slot):
        here = pl.ds(pl.multiple_of(part * unit, 8), unit)
        if slot == 0:
            src, dst, peer = by_row.at[pl.ds(0, 2), here, :], high_again.at[:, here, :], below
        else:
            src, dst, peer = by_row.at[pl.ds(rows - 2, 2), here, :], low_again.at[:, here, :], above
        return remote(src, dst, again_send.at[slot, part], again_recv.at[slot, part], peer, "lat")

    def out_copy(part, t):
        here = pl.ds(pl.multiple_of(part * unit * rows, 8), unit * rows)
        return pltpu.make_async_copy(
            block.at[t, here, :], out_ref.at[here, pl.ds(t * TILE, TILE)], out_sem.at[part, t]
        )

    def rows_copy(at, which):
        here = pl.ds(pl.multiple_of((STEPS - LAST + at) * unit, 8), unit)
        there = pl.ds(pl.multiple_of(at * unit, 8), unit)
        src = (by_row, low_again, high_again)[which]
        dst = (rows_out, low_out, high_out)[which]
        return pltpu.make_async_copy(src.at[:, here, :], dst.at[:, there, :], rows_sem.at[at, which])

    def unpack(h, turn):
        for at, (which, part) in enumerate(QUEUE):
            if which == h and at > 1:

                @pl.when(turn == HOME[h][part])
                def _(at=at):
                    await_back(at)

        def unpack_step(i, carry):
            here = pl.ds(pl.multiple_of(turn * unit + i * 8, 8), 8)
            for t in range(across):
                turned = turn_blocks([returned[h, t * GROUP + q, here, :] for q in range(GROUP)])
                for at, row in enumerate(groups[h]):
                    by_row[row, here, t * TILE : (t + 1) * TILE] = turned[at]
            return carry

        lax.fori_loop(0, unit // 8, unpack_step, 0)

    def home_part(turn, carry):
        @pl.when(turn >= LEAD)
        def _():
            part = turn - LEAD
            unpack(0, part)
            again_copy(part, 0).wait()
            again_copy(part, 1).wait()

            @pl.when(part < STEPS - LAST)
            def _():
                def home_step(i, carry):
                    start = part * unit + i * 8
                    here = pl.ds(pl.multiple_of(start, 8), 8)

                    def put(row, t, value):
                        there = pl.ds(start * rows + row, 8, stride=rows)
                        block[t, there, :] = value

                    advect(
                        fetch(here, low_again, high_again),
                        list(range(rows)),
                        coefs_at(start),
                        face,
                        half,
                        mask,
                        put,
                    )
                    return carry

                lax.fori_loop(0, unit // 8, home_step, 0)
                for t in range(across):
                    out_copy(part, t).start()

            @pl.when(part >= STEPS - LAST)
            def _():
                for which in range(3):
                    rows_copy(part - (STEPS - LAST), which).start()

        @pl.when(turn < STEPS)
        def _():
            unpack(1, turn)
            again_copy(turn, 0).start()
            again_copy(turn, 1).start()

        return carry

    await_back(1)
    lax.fori_loop(0, STEPS + LEAD, home_part, 0)
    for part in range(STEPS - LAST):
        for t in range(across):
            out_copy(part, t).wait()
    for at in range(LAST):
        for which in range(3):
            rows_copy(at, which).wait()
    for copy in field_copies:
        copy.wait()
    for copy in ocean_copies:
        copy.wait()


def settle_kernel(
    second_ref,
    stokes_ref,
    rows_ref,
    low_ref,
    high_ref,
    fields_ref,
    coefs_ref,
    second_out,
    stokes_out,
    held,
    planes,
    by_row,
    low,
    high,
    fields,
    coefs,
    done,
    first_sem,
    load_sem,
    store_sem,
    plane_load,
    plane_store,
    done_sem,
):
    band = lax.axis_index("lat")
    bands = lax.axis_size("lat")
    edges = (jnp.where(band > 0, F32(1.0), F32(0.0)), jnp.where(band < bands - 1, F32(1.0), F32(0.0)))
    rows, tail, cols = by_row.shape
    across = cols // TILE
    start = held.shape[0] // rows
    turns = tail // 8
    size = held.shape[0] // turns
    depth = planes.shape[0] // PLANES
    firsts = [
        pltpu.make_async_copy(src, dst, first_sem.at[i])
        for i, (src, dst) in enumerate(
            (
                (fields_ref, fields),
                (coefs_ref, coefs),
                (low_ref, low),
                (high_ref, high),
                (rows_ref, by_row),
            )
        )
    ]

    def held_load(i):
        here = pl.ds(pl.multiple_of(i * size, 8), size)
        return pltpu.make_async_copy(second_ref.at[here], held.at[here], load_sem.at[i])

    def held_store(i):
        here = pl.ds(pl.multiple_of(i * size, 8), size)
        return pltpu.make_async_copy(held.at[here], second_out.at[here], store_sem.at[i])

    def plane_in(i):
        here = pl.ds(i * depth, depth)
        return pltpu.make_async_copy(stokes_ref.at[here], planes.at[here], plane_load.at[i])

    def plane_back(i):
        here = pl.ds(i * depth, depth)
        return pltpu.make_async_copy(planes.at[here], stokes_out.at[here], plane_store.at[i])

    def done_store(i, t):
        src = pl.ds(pl.multiple_of(i * 8 * rows, 8), 8 * rows)
        dst = pl.ds(pl.multiple_of((start + i * 8) * rows, 8), 8 * rows)
        return pltpu.make_async_copy(
            done.at[t, src, :], second_out.at[dst, pl.ds(t * TILE, TILE)], done_sem.at[i, t]
        )

    for copy in firsts:
        copy.start()
    for i in range(turns):
        held_load(i).start()
    for i in range(PLANES):
        plane_in(i).start()
    for copy in firsts:
        copy.wait()

    def turn_step(i, carry):
        held_load(i).wait()
        held_store(i).start()
        here = pl.ds(pl.multiple_of(i * 8, 8), 8)

        def get(row, t):
            lanes = slice(t * TILE, (t + 1) * TILE)
            if row < 0:
                return edges[0] * low[row + 2, here, lanes]
            if row >= rows:
                return edges[1] * high[row - rows, here, lanes]
            return by_row[row, here, lanes]

        def put(row, t, value):
            done[t, pl.ds(i * 8 * rows + row, 8, stride=rows), :] = value

        advect(
            get,
            list(range(rows)),
            coefs[pl.ds(pl.multiple_of(start + i * 8, 8), 8), :],
            fields.at[0],
            fields.at[1],
            fields.at[2],
            put,
        )
        for t in range(across):
            done_store(i, t).start()
        plane_in(i).wait()
        plane_back(i).start()
        return carry

    lax.fori_loop(0, turns, turn_step, 0)
    for i in range(turns):
        held_store(i).wait()
        for t in range(across):
            done_store(i, t).wait()
    for i in range(PLANES):
        plane_back(i).wait()


def settle(second, stokes, by_row, low, high, fields, coefs):
    hbm = pl.BlockSpec(memory_space=pl.ANY)
    dma = pltpu.SemaphoreType.DMA
    rows, tail, cols = by_row.shape
    turns = tail // 8
    across = cols // TILE
    return pl.pallas_call(
        settle_kernel,
        out_shape=(
            jax.ShapeDtypeStruct(second.shape, F32),
            jax.ShapeDtypeStruct(stokes.shape, F32),
        ),
        in_specs=[hbm] * 7,
        out_specs=(hbm, hbm),
        scratch_shapes=[
            VMEM((second.shape[0] - tail * rows, cols), F32),
            VMEM(stokes.shape, F32),
            VMEM(by_row.shape, F32),
            VMEM(low.shape, F32),
            VMEM(high.shape, F32),
            VMEM(fields.shape, F32),
            VMEM(coefs.shape, F32),
            VMEM((across, tail * rows, TILE), F32),
            dma((5,)),
            dma((turns,)),
            dma((turns,)),
            dma((PLANES,)),
            dma((PLANES,)),
            dma((turns, across)),
        ],
        compiler_params=pltpu.CompilerParams(vmem_limit_bytes=58 * 1024 * 1024),
    )(second, stokes, by_row, low, high, fields, coefs)


def step_call(spectrum, sea_mask, current, plus, minus, source_map, coefs, drift_table, count, bands):
    local, rows, cols = spectrum.shape
    bins = local * count
    profiles = drift_table.shape[0]
    lats, lons = source_map.shape
    strip = cols // count
    each = strip // LANES
    pieces = cols // LANES
    tail = local // STEPS * LAST
    hbm = pl.BlockSpec(memory_space=pl.ANY)
    dma = pltpu.SemaphoreType.DMA
    forth = max(len(cuts) for cuts in FORTH) - 1
    home = max(len(cuts) for cuts in HOME) - 1
    return pl.pallas_call(
        functools.partial(step_kernel, count, bands),
        out_shape=(
            jax.ShapeDtypeStruct((local * rows, cols), F32),
            jax.ShapeDtypeStruct((profiles, lats, lons), F32),
            jax.ShapeDtypeStruct((rows, tail, cols), F32),
            jax.ShapeDtypeStruct((2, tail, cols), F32),
            jax.ShapeDtypeStruct((2, tail, cols), F32),
            jax.ShapeDtypeStruct((3, rows, cols), F32),
            jax.ShapeDtypeStruct((local, coefs.shape[1]), F32),
        ),
        in_specs=[pl.BlockSpec(memory_space=pltpu.HBM)] * 8,
        out_specs=(hbm,) * 7,
        scratch_shapes=[
            VMEM((cols // TILE, local * rows, TILE), F32),
            VMEM((rows, local, cols), F32),
            VMEM((2, pieces, local, TILE), F32),
            VMEM((2, each, bins, TILE), F32),
            VMEM((2, each, bins, TILE), F32),
            VMEM((2, pieces, local, TILE), F32),
            VMEM((bins, bins), jnp.bfloat16),
            VMEM((bins, bins), jnp.bfloat16),
            VMEM((bins, bins), jnp.bfloat16),
            VMEM((bins, 2 * each * TILE), jnp.bfloat16),
            VMEM((bins, 2 * each * TILE), jnp.bfloat16),
            VMEM((profiles, each * TILE), F32),
            VMEM((rows, cols), F32),
            VMEM((rows, cols), F32),
            VMEM((rows, cols), F32),
            VMEM((count, rows, TILE), F32),
            VMEM((2, local, cols), F32),
            VMEM((2, local, cols), F32),
            VMEM((2, local, cols), F32),
            VMEM((2, local, cols), F32),
            VMEM((rows + 2, strip + 16, profiles), F32),
            VMEM((4, rows, profiles), F32),
            VMEM((lats, TILE), jnp.int32),
            VMEM((profiles, lats, lons), F32),
            VMEM((local, coefs.shape[1]), F32),
            VMEM(coefs.shape, F32),
            VMEM(drift_table.shape, F32),
            VMEM(sea_mask.shape, jnp.int32),
            VMEM(current.shape, F32),
            VMEM(plus.shape, jnp.int32),
            VMEM(minus.shape, jnp.int32),
            VMEM(source_map.shape, jnp.int32),
            dma((LOADS, cols // TILE)),
            dma((8,)),
            dma((count,)),
            dma((count,)),
            dma((2,)),
            dma((2,)),
            dma((2, forth, count)),
            dma((2, forth, count)),
            dma((2, home, count)),
            dma((2, home, count)),
            dma((2, STEPS)),
            dma((2, STEPS)),
            dma((4,)),
            dma((4,)),
            dma((STEPS, cols // TILE)),
            dma((lats // 8,)),
            dma((LAST, 3)),
            dma((4,)),
        ],
        compiler_params=pltpu.CompilerParams(
            collective_id=0, has_side_effects=True, vmem_limit_bytes=58 * 1024 * 1024
        ),
    )(spectrum.reshape(local * rows, cols), sea_mask, current, plus, minus, source_map, coefs, drift_table)


def on_device_fast(spectrum, sea_mask, current, partner_plus, partner_minus, source_map):
    count = lax.axis_size("bins")
    bands = lax.axis_size("lat")
    along_x, along_y, strength, drift_table = fixed_tables()
    forth = np.maximum(along_y, 0.0) / 6.0
    back = np.minimum(along_y, 0.0) / 6.0
    coefs = np.stack(
        [
            along_x / 6.0,
            forth,
            -6.0 * forth - 2.0 * back,
            3.0 * forth - 3.0 * back,
            2.0 * forth + 6.0 * back,
            -back,
            strength,
            np.zeros_like(forth),
        ],
        axis=1,
    ).astype(np.float32)
    second, stokes = settle(*step_call(
        spectrum,
        sea_mask,
        current.T,
        partner_plus,
        partner_minus,
        source_map.T,
        jnp.asarray(coefs),
        jnp.asarray(drift_table),
        count,
        bands,
    ))
    lons, lats = source_map.shape
    return (second.reshape(spectrum.shape), jnp.swapaxes(stokes.reshape(2, LEV, lats, lons), 2, 3))


def on_device(spectrum, sea_mask, current, partner_plus, partner_minus, source_map):
    count = lax.axis_size("bins")
    bins, rows, cols = spectrum.shape
    bands = lax.axis_size("lat")
    lons, lats = source_map.shape
    strip = cols // count
    fits = (
        rows == 2 * GROUP
        and bins % (8 * STEPS) == 0
        and bins % (8 * LOADS) == 0
        and cols % TILE == 0
        and strip * count == cols
        and strip % LANES == 0
        and strip <= TILE
        and bins * count % TILE == 0
        and lats == 2 * rows
        and 2 * LEV % PLANES == 0
        and (STEPS - LAST) * rows % LAST == 0
        and PLANES == LAST * bins // (8 * STEPS)
        and lons == 2 * strip
        and lons <= TILE
        and count > 2
        and count & (count - 1) == 0
        and bands > 2
    )
    body = on_device_fast if fits else on_device_plain
    return body(spectrum, sea_mask, current, partner_plus, partner_minus, source_map)


def solution(mesh):
    return jax.shard_map(
        on_device,
        mesh=mesh,
        in_specs=(
            P("bins", "lat", None),
            P("lat", None),
            P("bins", "lat"),
            P(),
            P(),
            P("bins", "lat"),
        ),
        out_specs=(P("bins", "lat", None), P(None, None, "bins", "lat")),
        check_vma=False,
    )
```

```python
import functools
import math

import jax
import jax.numpy as jnp
import numpy as np
from jax import lax
from jax.experimental import pallas as pl
from jax.experimental.pallas import tpu as pltpu
from jax.sharding import PartitionSpec as P

NDIR = 36
NFREQ = 32
LEV = 64


HIGHEST = lax.Precision.HIGHEST


def extended(block, sides, width):
    for axis, dim in sides:
        count = lax.axis_size(axis)
        forward = [(i, i + 1) for i in range(count - 1)]
        backward = [(target, source) for source, target in forward]
        low = lax.ppermute(
            lax.slice_in_dim(block, block.shape[dim] - width, None, axis=dim), axis, forward
        )
        high = lax.ppermute(lax.slice_in_dim(block, 0, width, axis=dim), axis, backward)
        block = jnp.concatenate([low, block, high], axis=dim)
    return block


def bin_tables():
    dir_index = jnp.arange(NDIR, dtype=jnp.float32)
    freq_index = jnp.arange(NFREQ, dtype=jnp.float32)
    angles = 2.0 * math.pi * (dir_index + 0.5) / NDIR
    speeds = 0.12 + 0.25 * (NFREQ - 1 - freq_index) / (NFREQ - 1)
    along_x = jnp.repeat(speeds, NDIR) * jnp.tile(jnp.cos(angles), NFREQ)
    along_y = jnp.repeat(speeds, NDIR) * jnp.tile(jnp.sin(angles), NFREQ)
    strength = jnp.repeat(0.06 * (1.0 + freq_index / (NFREQ - 1)), NDIR)
    levels = jnp.arange(LEV, dtype=jnp.float32) + 0.5
    wavenumber = 0.02 * jnp.power(1.15, freq_index)
    decay = jnp.repeat(jnp.exp(-levels[:, None] * wavenumber[None, :]), NDIR, axis=1)
    amplitude = 2.0 / math.sqrt(NDIR * NFREQ)
    cosines = jnp.tile(jnp.cos(angles), NFREQ)
    sines = jnp.tile(jnp.sin(angles), NFREQ)
    drift_table = amplitude * jnp.concatenate(
        [decay * cosines[None, :], decay * sines[None, :]], axis=0
    )
    return (along_x, along_y, strength, drift_table)


def fixed_tables():
    dir_index = np.arange(NDIR, dtype=np.float32)
    freq_index = np.arange(NFREQ, dtype=np.float32)
    angles = 2.0 * math.pi * (dir_index + 0.5) / NDIR
    speeds = 0.12 + 0.25 * (NFREQ - 1 - freq_index) / (NFREQ - 1)
    along_x = np.repeat(speeds, NDIR) * np.tile(np.cos(angles), NFREQ)
    along_y = np.repeat(speeds, NDIR) * np.tile(np.sin(angles), NFREQ)
    strength = np.repeat(0.06 * (1.0 + freq_index / (NFREQ - 1)), NDIR)
    levels = np.arange(LEV, dtype=np.float32) + 0.5
    wavenumber = 0.02 * np.power(np.float32(1.15), freq_index)
    decay = np.repeat(np.exp(-levels[:, None] * wavenumber[None, :]), NDIR, axis=1)
    amplitude = 2.0 / math.sqrt(NDIR * NFREQ)
    cosines = np.tile(np.cos(angles), NFREQ)
    sines = np.tile(np.sin(angles), NFREQ)
    drift_table = amplitude * np.concatenate(
        [decay * cosines[None, :], decay * sines[None, :]], axis=0
    )
    tables = (along_x, along_y, strength, drift_table)
    return tuple(np.asarray(table, dtype=np.float32) for table in tables)


def cell_means(current_cells):
    lon_count = current_cells.shape[0] // 2
    lat_count = current_cells.shape[1] // 2
    return current_cells.reshape(lon_count, 2, lat_count, 2).mean(axis=(1, 3))


def face_fluxes(padded, velocity, dimension):
    face_count = padded.shape[dimension] - 3

    def section(low_edge):
        return lax.slice_in_dim(padded, low_edge, low_edge + face_count, axis=dimension)

    left_value = (-section(0) + 5.0 * section(1) + 2.0 * section(2)) / 6.0
    right_value = (2.0 * section(1) + 5.0 * section(2) - section(3)) / 6.0
    return jnp.maximum(velocity, 0.0) * left_value + jnp.minimum(velocity, 0.0) * right_value


def transport(padded_rows, zonal_flow, along_x, along_y, sea_cells):
    row_count = padded_rows.shape[1] - 4
    spectra = padded_rows[:, 2 : 2 + row_count, :]
    padded_cols = jnp.pad(spectra, ((0, 0), (0, 0), (2, 2)))
    zonal_padded = jnp.pad(zonal_flow, ((0, 0), (1, 1)))
    face_zonal = 0.5 * (zonal_padded[:, :-1] + zonal_padded[:, 1:])
    speed_x = along_x[:, None, None] + face_zonal[None, :, :]
    flux_x = face_fluxes(padded_cols, speed_x, 2)
    flux_y = face_fluxes(padded_rows, along_y[:, None, None], 1)
    change = flux_x[:, :, 1:] - flux_x[:, :, :-1] + flux_y[:, 1:, :] - flux_y[:, :-1, :]
    return sea_cells[None, :, :] * (spectra - change)


def spread_to_ocean(rim, source_map):
    row_count = rim.shape[1] - 2
    col_count = rim.shape[2] - 2
    result = jnp.zeros((rim.shape[0], 2 * col_count, 2 * row_count), jnp.float32)
    for offset in range(9):
        row_shift = offset // 3 - 1
        col_shift = offset % 3 - 1
        shifted = rim[
            :, 1 + row_shift : 1 + row_shift + row_count, 1 + col_shift : 1 + col_shift + col_count
        ]
        shifted = jnp.swapaxes(shifted, 1, 2)
        shifted = jnp.repeat(jnp.repeat(shifted, 2, axis=1), 2, axis=2)
        result = result + jnp.where(source_map[None, :, :] == offset, shifted, jnp.float32(0.0))
    return result


def on_device_plain(spectrum, sea_mask, current, partner_plus, partner_minus, source_map):
    along_x, along_y, strength, drift_table = bin_tables()
    bin_count = NDIR * NFREQ
    local_bins = spectrum.shape[0]
    first_bin = lax.axis_index("bins") * local_bins
    local_x = lax.dynamic_slice_in_dim(along_x, first_bin, local_bins)
    local_y = lax.dynamic_slice_in_dim(along_y, first_bin, local_bins)
    sea_cells = sea_mask.astype(jnp.float32)
    strip_flow = cell_means(current)
    zonal_flow = lax.all_gather(strip_flow, "bins", axis=0, tiled=True).T
    masked = spectrum * sea_cells[None, :, :]
    padded = extended(masked, (("lat", 1),), 2)
    after_first = transport(padded, zonal_flow, local_x, local_y, sea_cells)
    bin_ids = jnp.arange(bin_count, dtype=jnp.int32)
    plus_table = (partner_plus[:, None] == bin_ids[None, :]).astype(jnp.float32)
    minus_table = (partner_minus[:, None] == bin_ids[None, :]).astype(jnp.float32)
    contract_first = (((0,), (0,)), ((), ()))
    arrived = lax.all_to_all(after_first, "bins", split_axis=2, concat_axis=0, tiled=True)
    row_count = arrived.shape[1]
    col_count = arrived.shape[2]
    flat_rows = arrived.reshape(bin_count, row_count * col_count)
    plus_part = jnp.dot(plus_table, flat_rows, precision=HIGHEST)
    minus_part = jnp.dot(minus_table, flat_rows, precision=HIGHEST)
    source = strength[:, None] * (
        flat_rows * flat_rows * (plus_part + minus_part) - 2.0 * flat_rows * plus_part * minus_part
    )
    back = lax.dot_general(plus_table, source, contract_first, precision=HIGHEST) + lax.dot_general(
        minus_table, source, contract_first, precision=HIGHEST
    )
    middle = flat_rows + (source - 0.5 * back)
    drift_rows = jnp.dot(drift_table, middle, precision=HIGHEST)
    middle, drift_rows = (
        middle.reshape(bin_count, row_count, col_count),
        drift_rows.reshape(2 * LEV, row_count, col_count),
    )
    rim = extended(drift_rows, (("bins", 2), ("lat", 1)), 1)
    ocean = spread_to_ocean(rim, source_map)
    stokes = ocean.reshape(2, LEV, ocean.shape[1], ocean.shape[2])
    returned = lax.all_to_all(middle, "bins", split_axis=0, concat_axis=2, tiled=True)
    padded_again = extended(returned, (("lat", 1),), 2)
    second = transport(padded_again, zonal_flow, local_x, local_y, sea_cells)
    return (second, stokes)

MESH = pl.DeviceIdType.MESH
TILE = 128
GROUP = 8
LANES = TILE // GROUP
VMEM = pltpu.VMEM
LOADS = 3
STEPS = 9
LEAD = 2
FORTH = ((0, 1, 5, 9), (0, 4, 9))
HOME = ((0, 3, 6, 8, 9), (0, 3, 6, 9))
LAST = 1
CUTS = 4
PLANES = 2
QUEUE = ((0, 0), (0, 1), (1, 0), (1, 1), (1, 2), (0, 2), (0, 3))
AHEAD = 2


def order(count):
    return list(range(count // 2, count)) + list(range(1, count // 2)) + [0]
F32 = jnp.float32


def row_groups(rows):
    edge = rows // 4
    inner = list(range(edge, rows - edge))
    return inner, list(range(edge)) + list(range(rows - edge, rows))


def turn_blocks(tiles):
    lane = lax.broadcasted_iota(jnp.int32, tiles[0].shape, 1) // LANES
    tiles = list(tiles)
    step = 1
    while step < GROUP:
        clear = lax.rem(lane // step, 2) == 0
        for i in range(GROUP):
            if i & step:
                continue
            upper, lower = tiles[i], tiles[i + step]
            tiles[i] = jnp.where(clear, upper, pltpu.roll(lower, step * LANES, 1))
            tiles[i + step] = jnp.where(clear, pltpu.roll(upper, TILE - step * LANES, 1), lower)
        step *= 2
    return tiles


def advect(get, wanted, coefs, face_ref, half_ref, mask_ref, put):
    cols = face_ref.shape[1]
    across = cols // TILE
    lane = lax.broadcasted_iota(jnp.int32, (8, TILE), 1)
    at_first = lane == 0
    at_second = lane <= 1
    at_last = lane == TILE - 1
    coef = [jnp.broadcast_to(coefs[:, i : i + 1], (8, TILE)) for i in range(6)]
    for row in wanted:
        c = [get(row, t) for t in range(across)]
        one = [pltpu.roll(value, 1, 1) for value in c]
        two = [pltpu.roll(value, 2, 1) for value in c]
        back = [pltpu.roll(value, TILE - 1, 1) for value in c]
        flux = []
        for t in range(across):
            lanes = slice(t * TILE, (t + 1) * TILE)
            m1 = jnp.where(at_first, one[t - 1] if t else 0.0, one[t])
            m2 = jnp.where(at_second, two[t - 1] if t else 0.0, two[t])
            p1 = jnp.where(at_last, back[t + 1] if t + 1 < across else 0.0, back[t])
            speed = coef[0] + face_ref[row : row + 1, lanes]
            ahead = speed > 0.0
            part = 3.0 * jnp.where(ahead, m1, c[t]) - jnp.where(ahead, m2, p1)
            flux.append(speed * (part + 2.0 * (m1 + c[t])))
            if t + 1 == across:
                end_speed = coef[0] + half_ref[row : row + 1, lanes]
                end = end_speed * jnp.where(end_speed > 0.0, 5.0 * c[t] - m1, 2.0 * c[t])
        shifted = [pltpu.roll(value, TILE - 1, 1) for value in flux]
        for t in range(across):
            lanes = slice(t * TILE, (t + 1) * TILE)
            upper = jnp.where(at_last, shifted[t + 1] if t + 1 < across else end, shifted[t])
            along_y = (
                coef[1] * get(row - 2, t)
                + coef[2] * get(row - 1, t)
                + coef[3] * c[t]
                + coef[4] * get(row + 1, t)
                + coef[5] * get(row + 2, t)
            )
            put(row, t, mask_ref[row : row + 1, lanes] * (c[t] - ((upper - flux[t]) + along_y)))


def halves(value):
    high = value.astype(jnp.bfloat16)
    return high, (value - high.astype(F32)).astype(jnp.bfloat16)


def step_kernel(
    count,
    bands,
    x_ref,
    mask_hbm,
    current_hbm,
    plus_hbm,
    minus_hbm,
    source_hbm,
    table_hbm,
    drift_hbm,
    out_ref,
    stokes_ref,
    rows_out,
    low_out,
    high_out,
    fields_out,
    coefs_out,
    block,
    by_row,
    leaving,
    arrived,
    middle,
    returned,
    plus_table,
    minus_table,
    back_table,
    parts,
    source_parts,
    total,
    mask,
    half,
    face,
    strips,
    low_halo,
    high_halo,
    low_again,
    high_again,
    near,
    columns,
    chosen_map,
    ocean,
    coefs,
    table,
    drift_ref,
    mask_ref,
    current_ref,
    plus_ref,
    minus_ref,
    source_ref,
    load_sem,
    table_sem,
    strip_send,
    strip_recv,
    halo_send,
    halo_recv,
    in_send,
    in_recv,
    back_send,
    back_recv,
    again_send,
    again_recv,
    near_send,
    near_recv,
    out_sem,
    ocean_sem,
    rows_sem,
    fields_sem,
):
    me = lax.axis_index("bins")
    band = lax.axis_index("lat")
    rows, local, cols = by_row.shape
    bins = local * count
    strip = cols // count
    each = strip // LANES
    pieces = cols // LANES
    unit = local // STEPS
    tiles = bins // TILE
    width = each * TILE
    across = cols // TILE
    groups = row_groups(rows)
    below = lax.rem(band + bands - 1, bands)
    above = lax.rem(band + 1, bands)
    left = lax.rem(me + count - 1, count)
    right = lax.rem(me + 1, count)
    edges = (jnp.where(band > 0, F32(1.0), F32(0.0)), jnp.where(band < bands - 1, F32(1.0), F32(0.0)))

    def remote(src, dst, send_sem, recv_sem, peer, axis="bins"):
        return pltpu.make_async_remote_copy(
            src_ref=src,
            dst_ref=dst,
            send_sem=send_sem,
            recv_sem=recv_sem,
            device_id={axis: peer},
            device_id_type=MESH,
        )

    chunk_load = local // LOADS

    def load_copy(part, t):
        here = pl.ds(part * chunk_load * rows, chunk_load * rows)
        return pltpu.make_async_copy(
            x_ref.at[here, pl.ds(t * TILE, TILE)], block.at[t, here, :], load_sem.at[part, t]
        )

    first_bin = me * local
    own_bins = pl.ds(pl.multiple_of(first_bin, 8), local)
    table_copies = [
        pltpu.make_async_copy(src, dst, table_sem.at[i])
        for i, (src, dst) in enumerate(
            (
                (current_hbm, current_ref),
                (mask_hbm, mask_ref),
                (table_hbm.at[own_bins], coefs),
                (table_hbm, table),
                (drift_hbm, drift_ref),
                (plus_hbm, plus_ref),
                (minus_hbm, minus_ref),
                (source_hbm, source_ref),
            )
        )
    ]
    for copy in table_copies[:2]:
        copy.start()
    for part in range(LOADS):
        for t in range(across):
            load_copy(part, t).start()

    near[...] = jnp.zeros_like(near)
    barrier = pltpu.get_barrier_semaphore()
    for step in range(1, count):
        pl.semaphore_signal(
            barrier,
            inc=1,
            device_id={"bins": lax.rem(me + step, count)},
            device_id_type=MESH,
        )
    for peer in (below, above):
        pl.semaphore_signal(barrier, inc=1, device_id={"lat": peer}, device_id_type=MESH)

    lons = current_ref.shape[1]
    for copy in table_copies[:2]:
        copy.wait()
    pairs = current_ref[pl.ds(0, rows, stride=2), :] + current_ref[pl.ds(1, rows, stride=2), :]
    fold = lax.broadcasted_iota(jnp.int32, (lons, TILE), 0) // 2
    fold = jnp.where(fold == lax.broadcasted_iota(jnp.int32, (lons, TILE), 1), F32(0.125), F32(0.0))
    strips[me] = jnp.dot(pairs, fold, precision=HIGHEST, preferred_element_type=F32)
    mask[...] = mask_ref[...].astype(F32)

    pl.semaphore_wait(barrier, count + 1)

    def strip_copy(step):
        peer = lax.rem(me + step, count)
        return remote(strips.at[me], strips.at[me], strip_send.at[step], strip_recv.at[step], peer)

    for step in range(1, count):
        strip_copy(step).start()

    for part in range(LOADS):
        for t in range(across):
            load_copy(part, t).wait()

        def turn_step(i, carry, part=part):
            here = pl.ds(pl.multiple_of(part * chunk_load + i * 8, 8), 8)
            start = (part * chunk_load + i * 8) * rows
            for row in range(rows):
                there = pl.ds(start + row, 8, stride=rows)
                for t in range(across):
                    lanes = slice(t * TILE, (t + 1) * TILE)
                    by_row[row, here, lanes] = block[t, there, :] * mask[row : row + 1, lanes]
            return carry

        lax.fori_loop(0, chunk_load // 8, turn_step, 0)

    halo_copies = [
        remote(
            by_row.at[pl.ds(0, 2)], high_halo, halo_send.at[0], halo_recv.at[0], below, "lat"
        ),
        remote(
            by_row.at[pl.ds(rows - 2, 2)], low_halo, halo_send.at[1], halo_recv.at[1], above, "lat"
        ),
    ]
    for copy in halo_copies + table_copies[2:]:
        copy.start()
    table_copies[2].wait()
    for step in range(1, count):
        strip_copy(step).wait()
    spread = jnp.zeros((rows, cols), F32)
    rest = jnp.zeros((rows, cols - TILE), F32)
    for peer in range(count):
        piece = jnp.concatenate([strips[peer], rest], axis=1)
        spread = spread + (pltpu.roll(piece, peer * strip, 1) if peer else piece)
    spread = spread * F32(1.0 / 6.0)
    half[...] = spread
    first_lane = lax.broadcasted_iota(jnp.int32, (rows, cols), 1) == 0
    face[...] = spread + jnp.where(first_lane, 0.0, pltpu.roll(spread, 1, 1))
    field_copies = [
        pltpu.make_async_copy(src, dst, fields_sem.at[i])
        for i, (src, dst) in enumerate(
            (
                (face, fields_out.at[0]),
                (half, fields_out.at[1]),
                (mask, fields_out.at[2]),
                (coefs, coefs_out),
            )
        )
    ]

    def fetch(here, low, high):
        def get(row, t):
            lanes = slice(t * TILE, (t + 1) * TILE)
            if row < 0:
                return edges[0] * low[row + 2, here, lanes]
            if row >= rows:
                return edges[1] * high[row - rows, here, lanes]
            return by_row[row, here, lanes]

        return get

    def coefs_at(start):
        return coefs[pl.ds(pl.multiple_of(start, 8), 8), :]

    def flip(step):
        peer = me
        weight = 1
        while weight < count:
            if step & weight:
                peer = peer + weight - 2 * weight * lax.rem(me // weight, 2)
            weight *= 2
        return peer

    def reach(cuts, part):
        return cuts[part] * unit, (cuts[part + 1] - cuts[part]) * unit

    def in_copy(h, part, step):
        peer = flip(step)
        at, size = reach(FORTH[h], part)
        src = leaving.at[h, pl.ds(peer * each, each), pl.ds(at, size), :]
        dst = arrived.at[h, :, pl.ds(pl.multiple_of(first_bin + at, 8), size), :]
        if step == 0:
            return pltpu.make_async_copy(src, dst, in_recv.at[h, part, 0])
        return remote(src, dst, in_send.at[h, part, step], in_recv.at[h, part, step], peer)

    for h in range(2):
        if h == 1:
            for copy in halo_copies:
                copy.wait()

        def forth_turn(turn, carry, h=h):
            def forth_step(i, carry):
                start = turn * unit + i * 8
                here = pl.ds(pl.multiple_of(start, 8), 8)
                found = {}
                advect(
                    fetch(here, low_halo, high_halo),
                    groups[h],
                    coefs_at(start),
                    face,
                    half,
                    mask,
                    lambda row, t, value: found.update({(row, t): value}),
                )
                for t in range(across):
                    turned = turn_blocks([found[row, t] for row in groups[h]])
                    for q in range(GROUP):
                        leaving[h, t * GROUP + q, here, :] = turned[q]
                return carry

            lax.fori_loop(0, unit // 8, forth_step, 0)
            for part, end in enumerate(FORTH[h][1:]):

                @pl.when(turn == end - 1)
                def _(part=part):
                    for step in order(count):
                        in_copy(h, part, step).start()

            return carry

        lax.fori_loop(0, STEPS, forth_turn, 0)

    def table_step(tile, carry):
        here = pl.ds(pl.multiple_of(tile * TILE, TILE), TILE)
        along = lax.broadcasted_iota(jnp.int32, (TILE, bins), 1).astype(F32)
        down = (lax.broadcasted_iota(jnp.int32, (TILE, bins), 0) + tile * TILE).astype(F32)
        one = F32(1.0)
        zero = F32(0.0)
        back = jnp.zeros((TILE, bins), F32)
        for partner_ref, picks in ((plus_ref, plus_table), (minus_ref, minus_table)):
            column = jnp.broadcast_to(partner_ref[here][None, :], (TILE, TILE)).astype(F32).T
            column = jnp.concatenate([column] * tiles, axis=1)
            picks[here, :] = jnp.where(column == along, one, zero).astype(jnp.bfloat16)
            whole = partner_ref[...][None, :].astype(F32)
            back = back + jnp.where(whole == down, one, zero)
        back_table[here, :] = back.astype(jnp.bfloat16)
        return carry

    for copy in field_copies:
        copy.start()
    for copy in table_copies[3:]:
        copy.wait()
    lax.fori_loop(0, tiles, table_step, 0)

    def back_copy(h, part, step):
        peer = flip(step)
        at, size = reach(HOME[h], part)
        src = middle.at[h, :, pl.ds(pl.multiple_of(peer * local + at, 8), size), :]
        dst = returned.at[h, pl.ds(me * each, each), pl.ds(at, size), :]
        if step == 0:
            return pltpu.make_async_copy(src, dst, back_recv.at[h, part, 0])
        return remote(src, dst, back_send.at[h, part, step], back_recv.at[h, part, step], peer)

    def send_back(at):
        for step in order(count):
            back_copy(*QUEUE[at], step).start()

    def await_back(at):
        for step in range(count):
            back_copy(*QUEUE[at], step).wait()
        if at + AHEAD < len(QUEUE):
            send_back(at + AHEAD)

    def pick(table, here, value):
        both = jnp.dot(table[here, :], value[...], preferred_element_type=F32)
        return both[:, :width] + both[:, width:]

    def near_copy(slot):
        if slot == 0:
            src, dst, peer, axis = columns.at[0], columns.at[2], left, "bins"
        elif slot == 1:
            src, dst, peer, axis = columns.at[1], columns.at[3], right, "bins"
        elif slot == 2:
            src, dst, peer, axis = near.at[1], near.at[rows + 1], below, "lat"
        else:
            src, dst, peer, axis = near.at[rows], near.at[0], above, "lat"
        return remote(src, dst, near_send.at[slot], near_recv.at[slot], peer, axis)

    for h in range(2):
        for part in range(len(FORTH[h]) - 1):
            for step in range(count):
                in_copy(h, part, step).wait()

        def split_step(tile, carry, h=h):
            here = pl.ds(pl.multiple_of(tile * TILE, TILE), TILE)
            for g in range(each):
                upper, lower = halves(arrived[h, g, here, :])
                parts[here, g * TILE : (g + 1) * TILE] = upper
                parts[here, width + g * TILE : width + (g + 1) * TILE] = lower
            return carry

        lax.fori_loop(0, tiles, split_step, 0)

        def source_step(tile, carry, h=h):
            here = pl.ds(pl.multiple_of(tile * TILE, TILE), TILE)
            plus = pick(plus_table, here, parts)
            minus = pick(minus_table, here, parts)
            strength = table[here, 6:7]
            for g in range(each):
                lanes = slice(g * TILE, (g + 1) * TILE)
                own = arrived[h, g, here, :]
                p, m = plus[:, lanes], minus[:, lanes]
                source = strength * (own * own * (p + m) - 2.0 * own * p * m)
                upper, lower = halves(source)
                source_parts[here, lanes] = upper
                source_parts[here, width + g * TILE : width + (g + 1) * TILE] = lower
                middle[h, g, here, :] = own + source
            return carry

        lax.fori_loop(0, tiles, source_step, 0)
        total[...] = jnp.zeros_like(total)

        def back_step(tile, carry, h=h):
            here = pl.ds(pl.multiple_of(tile * TILE, TILE), TILE)
            back = pick(back_table, here, source_parts)
            done = []
            for g in range(each):
                value = middle[h, g, here, :] - 0.5 * back[:, g * TILE : (g + 1) * TILE]
                middle[h, g, here, :] = value
                done.append(value)
            total[...] += jnp.dot(
                drift_ref[:, here],
                jnp.concatenate(done, axis=1),
                precision=HIGHEST,
                preferred_element_type=F32,
            )
            return carry

        lax.fori_loop(0, tiles, back_step, 0)
        for g in range(each):
            points = total[:, g * TILE : (g + 1) * TILE].T
            for at, row in enumerate(groups[h]):
                near[1 + row, 8 + g * LANES : 8 + (g + 1) * LANES, :] = points[at * LANES : (at + 1) * LANES, :]
        if h == 1:
            for row in range(rows):
                columns[0, row : row + 1, :] = near[1 + row, 8:9, :]
                columns[1, row : row + 1, :] = near[1 + row, 7 + strip : 8 + strip, :]
            near_copy(0).start()
            near_copy(1).start()

        for at, (which, part) in enumerate(QUEUE[:AHEAD]):
            if which == h:
                send_back(at)

    await_back(0)
    near_copy(0).wait()
    near_copy(1).wait()
    side = (jnp.where(me > 0, F32(1.0), F32(0.0)), jnp.where(me < count - 1, F32(1.0), F32(0.0)))
    for row in range(rows):
        near[1 + row, 7:8, :] = columns[3, row : row + 1, :] * side[0]
        near[1 + row, 8 + strip : 9 + strip, :] = columns[2, row : row + 1, :] * side[1]
    near_copy(2).start()
    near_copy(3).start()

    chosen_map[...] = jnp.zeros_like(chosen_map)
    sources = source_ref[...]
    third = jnp.where(sources >= 3, 1, 0) + jnp.where(sources >= 6, 1, 0)
    extent = strip + 16
    column = lax.broadcasted_iota(jnp.int32, sources.shape, 1) // 2
    chosen_map[:, :lons] = third * extent + 7 + column + (sources - 3 * third)
    near_copy(2).wait()
    near_copy(3).wait()
    near[0] = near[0] * edges[0]
    near[rows + 1] = near[rows + 1] * edges[1]

    depth = 3 * extent
    profiles = near.shape[2]
    ocean_copies = []
    for octet in range(2 * rows // 8):
        found = []
        for row in range(octet * 4, octet * 4 + 4):
            window = near[row : row + 3].reshape(depth, profiles)
            down = lax.broadcasted_iota(jnp.int32, (depth, TILE), 0)
            chosen = [
                jnp.where(down == chosen_map[lat : lat + 1, :], F32(1.0), F32(0.0))
                for lat in (2 * row, 2 * row + 1)
            ]
            both = lax.dot_general(
                window,
                jnp.concatenate(chosen, axis=1),
                (((0,), (0,)), ((), ())),
                precision=HIGHEST,
                preferred_element_type=F32,
            )
            found += [both[:, :TILE], both[:, TILE:]]
        here = pl.ds(octet * 8, 8)
        ocean[:, here, :] = pltpu.einshape("ypl->pyl", jnp.stack(found))[:, :, :lons]
        copy = pltpu.make_async_copy(ocean.at[:, here, :], stokes_ref.at[:, here, :], ocean_sem.at[octet])
        copy.start()
        ocean_copies.append(copy)

    def again_copy(part, slot):
        here = pl.ds(pl.multiple_of(part * unit, 8), unit)
        if slot == 0:
            src, dst, peer = by_row.at[pl.ds(0, 2), here, :], high_again.at[:, here, :], below
        else:
            src, dst, peer = by_row.at[pl.ds(rows - 2, 2), here, :], low_again.at[:, here, :], above
        return remote(src, dst, again_send.at[slot, part], again_recv.at[slot, part], peer, "lat")

    def out_copy(part, t):
        here = pl.ds(pl.multiple_of(part * unit * rows, 8), unit * rows)
        return pltpu.make_async_copy(
            block.at[t, here, :], out_ref.at[here, pl.ds(t * TILE, TILE)], out_sem.at[part, t]
        )

    def rows_copy(at, which):
        here = pl.ds(pl.multiple_of((STEPS - LAST + at) * unit, 8), unit)
        there = pl.ds(pl.multiple_of(at * unit, 8), unit)
        src = (by_row, low_again, high_again)[which]
        dst = (rows_out, low_out, high_out)[which]
        return pltpu.make_async_copy(src.at[:, here, :], dst.at[:, there, :], rows_sem.at[at, which])

    def unpack(h, turn):
        for at, (which, part) in enumerate(QUEUE):
            if which == h and at > 1:

                @pl.when(turn == HOME[h][part])
                def _(at=at):
                    await_back(at)

        def unpack_step(i, carry):
            here = pl.ds(pl.multiple_of(turn * unit + i * 8, 8), 8)
            for t in range(across):
                turned = turn_blocks([returned[h, t * GROUP + q, here, :] for q in range(GROUP)])
                for at, row in enumerate(groups[h]):
                    by_row[row, here, t * TILE : (t + 1) * TILE] = turned[at]
            return carry

        lax.fori_loop(0, unit // 8, unpack_step, 0)

    def home_part(turn, carry):
        @pl.when(turn >= LEAD)
        def _():
            part = turn - LEAD
            unpack(0, part)
            again_copy(part, 0).wait()
            again_copy(part, 1).wait()

            @pl.when(part < STEPS - LAST)
            def _():
                def home_step(i, carry):
                    start = part * unit + i * 8
                    here = pl.ds(pl.multiple_of(start, 8), 8)

                    def put(row, t, value):
                        there = pl.ds(start * rows + row, 8, stride=rows)
                        block[t, there, :] = value

                    advect(
                        fetch(here, low_again, high_again),
                        list(range(rows)),
                        coefs_at(start),
                        face,
                        half,
                        mask,
                        put,
                    )
                    return carry

                lax.fori_loop(0, unit // 8, home_step, 0)
                for t in range(across):
                    out_copy(part, t).start()

            @pl.when(part >= STEPS - LAST)
            def _():
                for which in range(3):
                    rows_copy(part - (STEPS - LAST), which).start()

        @pl.when(turn < STEPS)
        def _():
            unpack(1, turn)
            again_copy(turn, 0).start()
            again_copy(turn, 1).start()

        return carry

    await_back(1)
    lax.fori_loop(0, STEPS + LEAD, home_part, 0)
    for part in range(STEPS - LAST):
        for t in range(across):
            out_copy(part, t).wait()
    for at in range(LAST):
        for which in range(3):
            rows_copy(at, which).wait()
    for copy in field_copies:
        copy.wait()
    for copy in ocean_copies:
        copy.wait()


def settle_kernel(
    second_ref,
    stokes_ref,
    rows_ref,
    low_ref,
    high_ref,
    fields_ref,
    coefs_ref,
    second_out,
    stokes_out,
    held,
    planes,
    by_row,
    low,
    high,
    fields,
    coefs,
    done,
    first_sem,
    load_sem,
    store_sem,
    plane_load,
    plane_store,
    done_sem,
):
    band = lax.axis_index("lat")
    bands = lax.axis_size("lat")
    edges = (jnp.where(band > 0, F32(1.0), F32(0.0)), jnp.where(band < bands - 1, F32(1.0), F32(0.0)))
    rows, tail, cols = by_row.shape
    across = cols // TILE
    start = held.shape[0] // rows
    turns = tail // 8
    size = held.shape[0] // (turns * CUTS)
    depth = planes.shape[0] // PLANES
    firsts = [
        pltpu.make_async_copy(src, dst, first_sem.at[i])
        for i, (src, dst) in enumerate(
            (
                (fields_ref, fields),
                (coefs_ref, coefs),
                (low_ref, low),
                (high_ref, high),
                (rows_ref, by_row),
            )
        )
    ]

    def held_load(i):
        here = pl.ds(pl.multiple_of(i * size, 8), size)
        return pltpu.make_async_copy(second_ref.at[here], held.at[here], load_sem.at[i])

    def held_store(i):
        here = pl.ds(pl.multiple_of(i * size, 8), size)
        return pltpu.make_async_copy(held.at[here], second_out.at[here], store_sem.at[i])

    def plane_in(i):
        here = pl.ds(i * depth, depth)
        return pltpu.make_async_copy(stokes_ref.at[here], planes.at[here], plane_load.at[i])

    def plane_back(i):
        here = pl.ds(i * depth, depth)
        return pltpu.make_async_copy(planes.at[here], stokes_out.at[here], plane_store.at[i])

    def done_store(i, t):
        src = pl.ds(pl.multiple_of(i * 8 * rows, 8), 8 * rows)
        dst = pl.ds(pl.multiple_of((start + i * 8) * rows, 8), 8 * rows)
        return pltpu.make_async_copy(
            done.at[t, src, :], second_out.at[dst, pl.ds(t * TILE, TILE)], done_sem.at[i, t]
        )

    for copy in firsts:
        copy.start()
    for i in range(turns * CUTS):
        held_load(i).start()
    for i in range(PLANES):
        plane_in(i).start()
    for copy in firsts:
        copy.wait()

    def turn_step(i, carry):
        for cut in range(CUTS):
            held_load(i * CUTS + cut).wait()
            held_store(i * CUTS + cut).start()
        here = pl.ds(pl.multiple_of(i * 8, 8), 8)

        def get(row, t):
            lanes = slice(t * TILE, (t + 1) * TILE)
            if row < 0:
                return edges[0] * low[row + 2, here, lanes]
            if row >= rows:
                return edges[1] * high[row - rows, here, lanes]
            return by_row[row, here, lanes]

        def put(row, t, value):
            done[t, pl.ds(i * 8 * rows + row, 8, stride=rows), :] = value

        advect(
            get,
            list(range(rows)),
            coefs[pl.ds(pl.multiple_of(start + i * 8, 8), 8), :],
            fields.at[0],
            fields.at[1],
            fields.at[2],
            put,
        )
        for t in range(across):
            done_store(i, t).start()
        plane_in(i).wait()
        plane_back(i).start()
        return carry

    lax.fori_loop(0, turns, turn_step, 0)
    for i in range(turns * CUTS):
        held_store(i).wait()
    for i in range(turns):
        for t in range(across):
            done_store(i, t).wait()
    for i in range(PLANES):
        plane_back(i).wait()


def settle(second, stokes, by_row, low, high, fields, coefs):
    hbm = pl.BlockSpec(memory_space=pl.ANY)
    dma = pltpu.SemaphoreType.DMA
    rows, tail, cols = by_row.shape
    turns = tail // 8
    across = cols // TILE
    return pl.pallas_call(
        settle_kernel,
        out_shape=(
            jax.ShapeDtypeStruct(second.shape, F32),
            jax.ShapeDtypeStruct(stokes.shape, F32),
        ),
        in_specs=[hbm] * 7,
        out_specs=(hbm, hbm),
        scratch_shapes=[
            VMEM((second.shape[0] - tail * rows, cols), F32),
            VMEM(stokes.shape, F32),
            VMEM(by_row.shape, F32),
            VMEM(low.shape, F32),
            VMEM(high.shape, F32),
            VMEM(fields.shape, F32),
            VMEM(coefs.shape, F32),
            VMEM((across, tail * rows, TILE), F32),
            dma((5,)),
            dma((turns * CUTS,)),
            dma((turns * CUTS,)),
            dma((PLANES,)),
            dma((PLANES,)),
            dma((turns, across)),
        ],
        compiler_params=pltpu.CompilerParams(vmem_limit_bytes=58 * 1024 * 1024),
    )(second, stokes, by_row, low, high, fields, coefs)


def step_call(spectrum, sea_mask, current, plus, minus, source_map, coefs, drift_table, count, bands):
    local, rows, cols = spectrum.shape
    bins = local * count
    profiles = drift_table.shape[0]
    lats, lons = source_map.shape
    strip = cols // count
    each = strip // LANES
    pieces = cols // LANES
    tail = local // STEPS * LAST
    hbm = pl.BlockSpec(memory_space=pl.ANY)
    dma = pltpu.SemaphoreType.DMA
    forth = max(len(cuts) for cuts in FORTH) - 1
    home = max(len(cuts) for cuts in HOME) - 1
    return pl.pallas_call(
        functools.partial(step_kernel, count, bands),
        out_shape=(
            jax.ShapeDtypeStruct((local * rows, cols), F32),
            jax.ShapeDtypeStruct((profiles, lats, lons), F32),
            jax.ShapeDtypeStruct((rows, tail, cols), F32),
            jax.ShapeDtypeStruct((2, tail, cols), F32),
            jax.ShapeDtypeStruct((2, tail, cols), F32),
            jax.ShapeDtypeStruct((3, rows, cols), F32),
            jax.ShapeDtypeStruct((local, coefs.shape[1]), F32),
        ),
        in_specs=[pl.BlockSpec(memory_space=pltpu.HBM)] * 8,
        out_specs=(hbm,) * 7,
        scratch_shapes=[
            VMEM((cols // TILE, local * rows, TILE), F32),
            VMEM((rows, local, cols), F32),
            VMEM((2, pieces, local, TILE), F32),
            VMEM((2, each, bins, TILE), F32),
            VMEM((2, each, bins, TILE), F32),
            VMEM((2, pieces, local, TILE), F32),
            VMEM((bins, bins), jnp.bfloat16),
            VMEM((bins, bins), jnp.bfloat16),
            VMEM((bins, bins), jnp.bfloat16),
            VMEM((bins, 2 * each * TILE), jnp.bfloat16),
            VMEM((bins, 2 * each * TILE), jnp.bfloat16),
            VMEM((profiles, each * TILE), F32),
            VMEM((rows, cols), F32),
            VMEM((rows, cols), F32),
            VMEM((rows, cols), F32),
            VMEM((count, rows, TILE), F32),
            VMEM((2, local, cols), F32),
            VMEM((2, local, cols), F32),
            VMEM((2, local, cols), F32),
            VMEM((2, local, cols), F32),
            VMEM((rows + 2, strip + 16, profiles), F32),
            VMEM((4, rows, profiles), F32),
            VMEM((lats, TILE), jnp.int32),
            VMEM((profiles, lats, lons), F32),
            VMEM((local, coefs.shape[1]), F32),
            VMEM(coefs.shape, F32),
            VMEM(drift_table.shape, F32),
            VMEM(sea_mask.shape, jnp.int32),
            VMEM(current.shape, F32),
            VMEM(plus.shape, jnp.int32),
            VMEM(minus.shape, jnp.int32),
            VMEM(source_map.shape, jnp.int32),
            dma((LOADS, cols // TILE)),
            dma((8,)),
            dma((count,)),
            dma((count,)),
            dma((2,)),
            dma((2,)),
            dma((2, forth, count)),
            dma((2, forth, count)),
            dma((2, home, count)),
            dma((2, home, count)),
            dma((2, STEPS)),
            dma((2, STEPS)),
            dma((4,)),
            dma((4,)),
            dma((STEPS, cols // TILE)),
            dma((lats // 8,)),
            dma((LAST, 3)),
            dma((4,)),
        ],
        compiler_params=pltpu.CompilerParams(
            collective_id=0, has_side_effects=True, vmem_limit_bytes=58 * 1024 * 1024
        ),
    )(spectrum.reshape(local * rows, cols), sea_mask, current, plus, minus, source_map, coefs, drift_table)


def on_device_fast(spectrum, sea_mask, current, partner_plus, partner_minus, source_map):
    count = lax.axis_size("bins")
    bands = lax.axis_size("lat")
    along_x, along_y, strength, drift_table = fixed_tables()
    forth = np.maximum(along_y, 0.0) / 6.0
    back = np.minimum(along_y, 0.0) / 6.0
    coefs = np.stack(
        [
            along_x / 6.0,
            forth,
            -6.0 * forth - 2.0 * back,
            3.0 * forth - 3.0 * back,
            2.0 * forth + 6.0 * back,
            -back,
            strength,
            np.zeros_like(forth),
        ],
        axis=1,
    ).astype(np.float32)
    second, stokes = settle(*step_call(
        spectrum,
        sea_mask,
        current.T,
        partner_plus,
        partner_minus,
        source_map.T,
        jnp.asarray(coefs),
        jnp.asarray(drift_table),
        count,
        bands,
    ))
    lons, lats = source_map.shape
    return (second.reshape(spectrum.shape), jnp.swapaxes(stokes.reshape(2, LEV, lats, lons), 2, 3))


def on_device(spectrum, sea_mask, current, partner_plus, partner_minus, source_map):
    count = lax.axis_size("bins")
    bins, rows, cols = spectrum.shape
    bands = lax.axis_size("lat")
    lons, lats = source_map.shape
    strip = cols // count
    fits = (
        rows == 2 * GROUP
        and bins % (8 * STEPS) == 0
        and bins % (8 * LOADS) == 0
        and cols % TILE == 0
        and strip * count == cols
        and strip % LANES == 0
        and strip <= TILE
        and bins * count % TILE == 0
        and lats == 2 * rows
        and 2 * LEV % PLANES == 0
        and (STEPS - LAST) * rows % (LAST * CUTS) == 0
        and PLANES == LAST * bins // (8 * STEPS)
        and lons == 2 * strip
        and lons <= TILE
        and count > 2
        and count & (count - 1) == 0
        and bands > 2
    )
    body = on_device_fast if fits else on_device_plain
    return body(spectrum, sea_mask, current, partner_plus, partner_minus, source_map)


def solution(mesh):
    return jax.shard_map(
        on_device,
        mesh=mesh,
        in_specs=(
            P("bins", "lat", None),
            P("lat", None),
            P("bins", "lat"),
            P(),
            P(),
            P("bins", "lat"),
        ),
        out_specs=(P("bins", "lat", None), P(None, None, "bins", "lat")),
        check_vma=False,
    )
```
